32 devices in a mesh: gx: 4 (over z), gy: 2 (over core), gz: 4 (over y, x).
Axes of the slice: x: 2, y: 2, z: 4, core: 2. Of those that a mesh axis runs over, the one named last changes fastest.
Arguments:
- permeability: float32 [3, 8, 16, 512], P(None, 'gx', 'gy', 'gz'), may hold values from 0.05 to 20
- sat_mean: float32 [8, 16, 512], P('gx', 'gy', 'gz'), may hold values from 0 to 1
- sat_slopes: float32 [9, 8, 16, 512], P(None, 'gx', 'gy', 'gz'), may hold values from -0.9 to 0.9
- rock_ids: int32 [8, 16, 512], P('gx', 'gy', 'gz'), may hold values from 0 to 3
- rock_table: float32 [2, 4], replicated, may hold values from 0.3 to 3
- well_cells: int32 [64], replicated, may hold values from 0 to 65535
- well_rates: int32 [64], replicated, may hold values from -8 to 8
Outputs:
- traces: float32 [3, 8, 16, 512], P(None, 'gx', 'gy', 'gz')
- fluxes: float32 [3, 8, 16, 512], P(None, 'gx', 'gy', 'gz')
- saturation: float32 [10, 8, 16, 512], P(None, 'gx', 'gy', 'gz')
The draws below stay inside these ranges and needn't reach their ends.
Inputs may be any that keep to these rules, and one draw needn't show every extreme that they name: `well_cells`: global cell index x 16 * 512 + y * 512 + z; several wells may share a cell.
All inputs are finite; a program needn't handle non-finite values.
Results may differ from the reference program's by a relative error of at most 0.0003.
Values sent between devices are 32-bit elements; how exact they have to be, the bound alone decides.
A program may use at most 64 MiB of HBM per device.

```python
import math
import jax
import jax.numpy as jnp
import numpy as np
from jax import lax

ITERS = 3
ROCKS = 4
MODES = 10
NX = 8
NY = 16
NZ = 512
WELLS = 64


def plant(drawn, rng, smallest, largest):
    longest = drawn.shape.index(max(drawn.shape))
    spots = []
    for shift in (0, 1):
        where = [jax.random.randint(jax.random.fold_in(rng, axis), (), 0, length) for axis, length in enumerate(drawn.shape)]
        where[longest] = (where[longest] + shift) % drawn.shape[longest]
        spots.append(tuple(where))
    return drawn.at[spots[0]].set(smallest).at[spots[1]].set(largest)


def shard_levels(rng, shape, pieces, smallest, high):
    gain = 1.0
    for dim, shards_of in pieces:
        steps = jax.random.uniform(jax.random.fold_in(jax.random.fold_in(rng, 6), dim), (shards_of,), jnp.float32, smallest / len(pieces), high / len(pieces))
        gain = gain * jnp.repeat(jnp.exp(steps), shape[dim] // shards_of).reshape((-1,) + (1,) * (len(shape) - 1 - dim))
    return gain


def noise(key, dims, width, limit, shards=(), held_as=jnp.bfloat16):
    loudness = shard_levels(key, dims, shards, -0.22, 0.18) if shards else 1.0
    values = jax.random.normal(key, dims, jnp.float32) * width * loudness
    return jnp.minimum(jnp.maximum(values, -limit), limit).astype(held_as)


def setup_inputs(seed: int = 0) -> dict:
    keys = jax.random.split(jax.random.key(seed), 8)
    permeability = jnp.clip(jnp.exp(math.log(20.0) - 5.9914645 * jax.random.uniform(keys[0], (3, NX, NY, NZ), jnp.float32) ** shard_levels(keys[0], (3, NX, NY, NZ), ((1, 4), (2, 2), (3, 4)), -0.2, 0.2)), 0.05, 20.0)
    sat_mean = jnp.clip(1.0 * jax.random.uniform(keys[1], (NX, NY, NZ), jnp.float32) ** shard_levels(keys[1], (NX, NY, NZ), ((0, 4), (1, 2), (2, 4)), -0.2, 0.2), 0.0, 1.0)
    sat_slopes = noise(keys[2], (MODES - 1, NX, NY, NZ), 0.15, 0.9, ((1, 4), (2, 2), (3, 4)), jnp.float32)
    rock_ids = plant(jax.random.randint(keys[3], (NX, NY, NZ), 0, ROCKS), jax.random.fold_in(keys[3], 1), 0, ROCKS - 1).astype(jnp.int32)
    rock_table = jnp.clip(jnp.exp(jax.random.uniform(keys[4], (2, ROCKS), jnp.float32, math.log(0.3), math.log(3.0))), 0.3, 3.0)
    well_cells = plant(jax.random.randint(keys[5], (WELLS,), 0, NX * NY * NZ), jax.random.fold_in(keys[5], 1), 0, (NX * NY * NZ) - 1).astype(jnp.int32)
    well_rates = plant(jax.random.randint(keys[6], (WELLS,), -8, 9), jax.random.fold_in(keys[6], 1), -8, 8).astype(jnp.int32)
    return {"permeability": permeability, "sat_mean": sat_mean, "sat_slopes": sat_slopes, "rock_ids": rock_ids, "rock_table": rock_table, "well_cells": well_cells, "well_rates": well_rates}


time_step = 0.05
rate_unit = 0.5
gravity_head = 2.0

def legendre(order, coord):
    centred = 2.0 * coord - 1.0
    if order == 0:
        return centred * 0.0 + 1.0
    if order == 1:
        return centred
    return 1.5 * centred * centred - 0.5

def legendre_slope(order, coord):
    centred = 2.0 * coord - 1.0
    if order == 0:
        return centred * 0.0
    if order == 1:
        return centred * 0.0 + 2.0
    return 6.0 * centred

def mode_product(mode_list, coords):
    return np.stack([legendre(m[0], coords[0]) * legendre(m[1], coords[1]) * legendre(m[2], coords[2]) for m in mode_list], 1)

def basis_tables():
    mode_list = [(0, 0, 0), (1, 0, 0), (0, 1, 0), (0, 0, 1), (2, 0, 0), (0, 2, 0), (0, 0, 2), (1, 1, 0), (1, 0, 1), (0, 1, 1)]
    gauss_points = np.array([0.5 - 0.5 * np.sqrt(0.6), 0.5, 0.5 + 0.5 * np.sqrt(0.6)])
    line_weights = np.array([5.0, 8.0, 5.0]) / 18.0
    cube_points = np.stack(np.meshgrid(gauss_points, gauss_points, gauss_points, indexing='ij'), 0).reshape(3, 27)
    cube_weights = np.outer(np.outer(line_weights, line_weights).reshape(9), line_weights).reshape(27)
    values = mode_product(mode_list, cube_points)
    slopes = []
    for d in range(3):
        columns = []
        for m in mode_list:
            factor = np.ones(27)
            for e in range(3):
                if e == d:
                    factor = factor * legendre_slope(m[e], cube_points[e])
                else:
                    factor = factor * legendre(m[e], cube_points[e])
            columns.append(factor)
        slopes.append(np.stack(columns, 1))
    square = np.stack(np.meshgrid(gauss_points, gauss_points, indexing='ij'), 0).reshape(2, 9)
    square_weights = np.outer(line_weights, line_weights).reshape(9)
    face_tables = []
    for d in range(3):
        others = [e for e in range(3) if e != d]
        face_pair = []
        for face_side in (0.0, 1.0):
            coords = [None, None, None]
            coords[d] = np.full(9, face_side)
            coords[others[0]] = square[0]
            coords[others[1]] = square[1]
            face_pair.append(mode_product(mode_list, coords))
        face_tables.append(face_pair)
    mass_diag = np.array([1.0 / ((2 * m[0] + 1) * (2 * m[1] + 1) * (2 * m[2] + 1)) for m in mode_list])
    return (values, slopes, cube_weights, cube_points, face_tables, square_weights, mass_diag)

def as_array(table):
    return jnp.asarray(table, dtype=jnp.float32)

def unit(axis_dim, sign):
    return tuple((sign if e == axis_dim else 0 for e in range(3)))

def window(padded, offset):
    size_x = padded.shape[1] - 2
    size_y = padded.shape[2] - 2
    size_z = padded.shape[3] - 2
    return padded[:, 1 + offset[0]:1 + offset[0] + size_x, 1 + offset[1]:1 + offset[1] + size_y, 1 + offset[2]:1 + offset[2] + size_z]

def pad_cells(field):
    return jnp.pad(field, ((0, 0), (1, 1), (1, 1), (1, 1)))

def gravity_of(axis_dim):
    return gravity_head if axis_dim == 2 else 0.0

def cell_mean(trace_pad, coef_pad, offset):
    conduct = window(coef_pad, offset)[0:3]
    total = 2.0 * (conduct[0] + conduct[1] + conduct[2])
    divisor = jnp.where(total > 0.0, total, 1.0)
    after_faces = window(trace_pad, offset)
    running = jnp.zeros_like(total)
    for d in range(3):
        prior = tuple((offset[e] - (1 if e == d else 0) for e in range(3)))
        running = running + conduct[d] * (after_faces[d] + window(trace_pad, prior)[d])
    return running / divisor

def apply_operator(trace_pad, coef_pad):
    own_coef = window(coef_pad, (0, 0, 0))
    own_traces = window(trace_pad, (0, 0, 0))
    center = cell_mean(trace_pad, coef_pad, (0, 0, 0))
    stacked = []
    for d in range(3):
        offset = unit(d, 1)
        beyond = window(coef_pad, offset)[d]
        stacked.append(own_coef[d] * (own_traces[d] - center) + beyond * (own_traces[d] - cell_mean(trace_pad, coef_pad, offset)))
    return jnp.stack(stacked)

def load_vector(coef_pad):
    own_coef = window(coef_pad, (0, 0, 0))
    stacked = []
    for d in range(3):
        beyond = window(coef_pad, unit(d, 1))
        stacked.append(own_coef[d] * own_coef[3] + beyond[d] * beyond[3] + gravity_of(d) * (beyond[d] - own_coef[d]))
    return jnp.stack(stacked)

def recover_fluxes(trace_pad, coef_pad):
    own_coef = window(coef_pad, (0, 0, 0))
    own_traces = window(trace_pad, (0, 0, 0))
    pressure = cell_mean(trace_pad, coef_pad, (0, 0, 0)) + own_coef[3]
    stacked = []
    for d in range(3):
        offset = unit(d, 1)
        beyond = window(coef_pad, offset)
        beyond_pressure = cell_mean(trace_pad, coef_pad, offset) + beyond[3]
        gravity = gravity_of(d)
        stacked.append(0.5 * (own_coef[d] * (pressure - own_traces[d] - gravity) + beyond[d] * (own_traces[d] - beyond_pressure - gravity)))
    return jnp.stack(stacked)

def precondition(resid, conduct):
    total = 2.0 * (conduct[0] + conduct[1] + conduct[2])
    return resid / (2.0 * conduct) + ((resid[0] + resid[1] + resid[2]) / (3.0 * total))[None]

def frac_flow(saturation, water_rel, oil_rel):
    clipped = jnp.clip(saturation, 0.0, 1.0)
    water = water_rel * clipped * clipped
    oil_part = oil_rel * (1.0 - clipped) * (1.0 - clipped)
    return water / (water + oil_part)

def rate_of(state_pad, flux_pad, source, water_rel, oil_rel):
    values, slopes, cube_weights, cube_points, face_tables, square_weights, mass_diag = basis_tables()
    high = lax.Precision.HIGHEST
    state = window(state_pad, (0, 0, 0))
    fluxes = window(flux_pad, (0, 0, 0))
    at_points = jnp.einsum('qm,mxyz->qxyz', as_array(values), state, precision=high)
    flowing = frac_flow(at_points, water_rel, oil_rel) * as_array(cube_weights)[:, None, None, None]
    face_weights = as_array(square_weights)[:, None, None, None]
    result = jnp.zeros_like(state)
    for d in range(3):
        before = window(flux_pad, unit(d, -1))[d]
        coord = as_array(cube_points[d])[:, None, None, None]
        speed = before[None] * (1.0 - coord) + fluxes[d][None] * coord
        result = result + jnp.einsum('qm,qxyz->mxyz', as_array(slopes[d]), flowing * speed, precision=high)
        lower_table = as_array(face_tables[d][0])
        upper_table = as_array(face_tables[d][1])
        next_state = window(state_pad, unit(d, 1))
        prior_state = window(state_pad, unit(d, -1))
        own_upper = jnp.einsum('pm,mxyz->pxyz', upper_table, state, precision=high)
        next_lower = jnp.einsum('pm,mxyz->pxyz', lower_table, next_state, precision=high)
        upwind = jnp.where(fluxes[d][None] > 0.0, own_upper, next_lower)
        outgoing = face_weights * fluxes[d][None] * frac_flow(upwind, water_rel, oil_rel)
        result = result - jnp.einsum('pm,pxyz->mxyz', upper_table, outgoing, precision=high)
        own_lower = jnp.einsum('pm,mxyz->pxyz', lower_table, state, precision=high)
        prior_upper = jnp.einsum('pm,mxyz->pxyz', upper_table, prior_state, precision=high)
        upwind = jnp.where(before[None] > 0.0, prior_upper, own_lower)
        incoming = face_weights * before[None] * frac_flow(upwind, water_rel, oil_rel)
        result = result + jnp.einsum('pm,pxyz->mxyz', lower_table, incoming, precision=high)
    wells_term = jnp.where(source > 0.0, source, source * frac_flow(state[0], water_rel, oil_rel))
    first_mode = (jnp.arange(state.shape[0]) == 0).astype(jnp.float32)
    result = result + first_mode[:, None, None, None] * wells_term[None]
    return result / as_array(mass_diag)[:, None, None, None]

def rock_lookup(rock_ids, rock_table):
    kinds = jnp.arange(rock_table.shape[1], dtype=jnp.int32)
    onehot = (rock_ids[None] == kinds[:, None, None, None]).astype(jnp.float32)
    water_rel = lax.optimization_barrier(jnp.sum(rock_table[0][:, None, None, None] * onehot, 0))
    oil_rel = lax.optimization_barrier(jnp.sum(rock_table[1][:, None, None, None] * onehot, 0))
    return (water_rel, oil_rel)

def conductances(permeability, sat_mean, water_rel, oil_rel):
    clipped = jnp.clip(sat_mean, 0.0, 1.0)
    mobility = water_rel * clipped * clipped + oil_rel * (1.0 - clipped) * (1.0 - clipped)
    return 2.0 * permeability * mobility[None]

def global_rate(state, fluxes, source, water_rel, oil_rel):
    state_pad = pad_cells(state)
    flux_pad = pad_cells(fluxes)

    def one_slab(position):
        slab_state = lax.dynamic_slice_in_dim(state_pad, position, 3, 1)
        slab_flux = lax.dynamic_slice_in_dim(flux_pad, position, 3, 1)
        slab_source = lax.dynamic_slice_in_dim(source, position, 1, 0)
        slab_water = lax.dynamic_slice_in_dim(water_rel, position, 1, 0)
        slab_oil = lax.dynamic_slice_in_dim(oil_rel, position, 1, 0)
        return rate_of(slab_state, slab_flux, slab_source, slab_water, slab_oil)[:, 0]
    slabs = lax.map(one_slab, jnp.arange(NX, dtype=jnp.int32))
    return jnp.moveaxis(slabs, 0, 1)

def reference(permeability, sat_mean, sat_slopes, rock_ids, rock_table, well_cells, well_rates):
    state = jnp.concatenate([sat_mean[None], sat_slopes], 0)
    water_rel, oil_rel = rock_lookup(rock_ids, rock_table)
    conduct = conductances(permeability, sat_mean, water_rel, oil_rel)
    total = 2.0 * (conduct[0] + conduct[1] + conduct[2])
    flat = jnp.zeros((NX * NY * NZ,), jnp.float32).at[well_cells].add(well_rates.astype(jnp.float32) * rate_unit)
    source = flat.reshape(NX, NY, NZ)
    coef_pad = pad_cells(jnp.concatenate([conduct, (source / total)[None]], 0))
    resid = load_vector(coef_pad)
    traces = jnp.zeros_like(resid)
    precond = precondition(resid, conduct)
    image = apply_operator(pad_cells(precond), coef_pad)
    gamma = jnp.sum(resid * precond)
    delta = jnp.sum(image * precond)
    alpha = gamma / delta
    direction, along = (precond, image)
    for k in range(ITERS):
        traces = traces + alpha * direction
        resid = resid - alpha * along
        if k + 1 < ITERS:
            precond = precondition(resid, conduct)
            image = apply_operator(pad_cells(precond), coef_pad)
            gamma_new = jnp.sum(resid * precond)
            delta = jnp.sum(image * precond)
            beta = gamma_new / gamma
            alpha = gamma_new / (delta - beta * gamma_new / alpha)
            direction = precond + beta * direction
            along = image + beta * along
            gamma = gamma_new
    fluxes = recover_fluxes(pad_cells(traces), coef_pad)
    first = state + time_step * global_rate(state, fluxes, source, water_rel, oil_rel)
    second = 0.75 * state + 0.25 * (first + time_step * global_rate(first, fluxes, source, water_rel, oil_rel))
    saturation = state / 3.0 + 2.0 / 3.0 * (second + time_step * global_rate(second, fluxes, source, water_rel, oil_rel))
    return (traces, fluxes, saturation)
```

```python
import functools
import itertools

import jax
import jax.numpy as jnp
import numpy as np
from jax import lax
from jax.experimental import pallas as pl
from jax.experimental.pallas import tpu as pltpu
from jax.sharding import PartitionSpec as P

ITERS = 3
STEP = 0.05
GRAVITY = (0.0, 0.0, 2.0)
SHIFT = 0.6
ROUTE = (2, 0, 1)
ARRIVAL = (1, 0, 2)
AXES = ("gx", "gy", "gz")
MESH = pl.DeviceIdType.MESH
ROOT = float(np.sqrt(0.6))
XI = (-ROOT, 0.0, ROOT)
LEG2 = (0.4, -0.5, 0.4)
WEIGHT = (5.0 / 18.0, 8.0 / 18.0, 5.0 / 18.0)

LIN = (1, 2, 3)
SQR = (4, 5, 6)
MIX = {(0, 1): 7, (0, 2): 8, (1, 2): 9}
MASS = (1.0, 3.0, 3.0, 3.0, 5.0, 5.0, 5.0, 9.0, 9.0, 9.0)


def mix(a, b):
    return MIX[(min(a, b), max(a, b))]


def others(d):
    return [e for e in range(3) if e != d]


DIAGONALS = ((0, 2), (2, 0), (1, 2), (2, 1), (0, 1), (1, 0))


def message_list():
    names = {}
    order = []

    def add(key, dim, direction, fields):
        names[key] = len(order)
        order.append((dim, direction, fields))

    for d in range(3):
        add(("coef", d), d, -1, 4)
        add(("prior", d), d, 1, 2)
    for k in range(ITERS):
        for d in range(3):
            add(("vec", k, d), d, 1, 1)
        for d in range(3):
            add(("mean", k, d), d, -1, 1)
            add(("back", k, d), d, 1, 1)
        for d, e in DIAGONALS if k + 1 < ITERS else ():
            add(("diag", k, d, e), (d, e), None, 1)
    for s in range(3):
        for d in range(3):
            add(("up", s, d), d, 1, 6)
            add(("down", s, d), d, -1, 6)
    return names, order


NAMES, ORDER = message_list()
DIRECT = 64


def sum_phases(counts):
    split = [d for d in range(3) if counts[d] > 1]
    if int(np.prod(counts)) <= DIRECT:
        return [tuple(split)] if split else []
    return [(d,) for d in (1, 2, 0) if counts[d] > 1]


def peers(dims, counts):
    steps = itertools.product(*[range(counts[d]) for d in dims])
    return [dict(zip(dims, s)) for s in steps if any(s)]


def frac(sat, water, oil):
    c = jnp.clip(sat, 0.0, 1.0)
    w = water * c * c
    r = 1.0 - c
    return w * pl.reciprocal(w + oil * r * r, approx=True)


def trace(state, d, sign):
    e, f = others(d)
    return [
        (state[0] + state[SQR[d]]) + sign * state[LIN[d]],
        state[LIN[e]] + sign * state[mix(d, e)],
        state[LIN[f]] + sign * state[mix(d, f)],
        state[SQR[e]],
        state[SQR[f]],
        state[mix(e, f)],
    ]


def square_moments(coefs, water, oil):
    base, s, t, ss, tt, st = coefs
    firsts, seconds, thirds = [], [], []
    for i in range(3):
        if i == 1:
            a = base + LEG2[1] * ss
            b = t
        else:
            a = base + XI[i] * s + LEG2[i] * ss
            b = t + XI[i] * st
        outer = a + LEG2[0] * tt
        lean = ROOT * b
        low = frac(outer - lean, water, oil)
        mid = frac(a + LEG2[1] * tt, water, oil)
        high = frac(outer + lean, water, oil)
        both = low + high
        firsts.append(WEIGHT[0] * both + WEIGHT[1] * mid)
        seconds.append((WEIGHT[0] * ROOT) * (high - low))
        thirds.append((WEIGHT[0] * LEG2[0]) * both + (WEIGHT[1] * LEG2[1]) * mid)
    ends = firsts[0] + firsts[2]
    m00 = WEIGHT[0] * ends + WEIGHT[1] * firsts[1]
    m10 = (WEIGHT[0] * ROOT) * (firsts[2] - firsts[0])
    m20 = (WEIGHT[0] * LEG2[0]) * ends + (WEIGHT[1] * LEG2[1]) * firsts[1]
    m01 = WEIGHT[0] * (seconds[0] + seconds[2]) + WEIGHT[1] * seconds[1]
    m11 = (WEIGHT[0] * ROOT) * (seconds[2] - seconds[0])
    m02 = WEIGHT[0] * (thirds[0] + thirds[2]) + WEIGHT[1] * thirds[1]
    return m00, m10, m01, m20, m02, m11


def cube_moments(state, water, oil):
    c0, cx, cy, cz, cxx, cyy, czz, cxy, cxz, cyz = state
    w, v, q = WEIGHT[0], WEIGHT[1], WEIGHT[0] * 0.6
    planes = []
    for i in range(3):
        if i == 1:
            a = c0 + LEG2[1] * cxx
            by, bz = cy, cz
        else:
            a = c0 + XI[i] * cx + LEG2[i] * cxx
            by = cy + XI[i] * cxy
            bz = cz + XI[i] * cxz
        rows = []
        for j in range(3):
            if j == 1:
                b = a + LEG2[1] * cyy
                g = bz
            else:
                b = a + XI[j] * by + LEG2[j] * cyy
                g = bz + XI[j] * cyz
            edge = b + LEG2[0] * czz
            lean = ROOT * g
            low = frac(edge - lean, water, oil)
            mid = frac(b + LEG2[1] * czz, water, oil)
            high = frac(edge + lean, water, oil)
            both = low + high
            rows.append((w * both + v * mid, (w * ROOT) * (high - low), q * both))
        r0, r1, r2 = zip(*rows)
        planes.append(
            (
                w * (r0[0] + r0[2]) + v * r0[1],
                (w * ROOT) * (r0[2] - r0[0]),
                q * (r0[0] + r0[2]),
                w * (r1[0] + r1[2]) + v * r1[1],
                (w * ROOT) * (r1[2] - r1[0]),
                w * (r2[0] + r2[2]) + v * r2[1],
            )
        )
    p00, p10, p20, p01, p11, p02 = zip(*planes)

    def even(p):
        return w * (p[0] + p[2]) + v * p[1]

    def odd(p):
        return (w * ROOT) * (p[2] - p[0])

    m1 = even(p00)
    mlin = (odd(p00), even(p10), even(p01))
    msqr = (q * (p00[0] + p00[2]), even(p20), even(p02))
    mmix = {(0, 1): odd(p10), (0, 2): odd(p01), (1, 2): even(p11)}
    return m1, mlin, msqr, mmix


def is_packed(dim, fields, tile):
    return dim == 2 and fields > 2 and fields * tile[0] < tile[2]


def buffer_shape(dim, fields, tile):
    if is_packed(dim, fields, tile):
        return (1, 1, tile[1], tile[2])
    flat = 0 in dim if isinstance(dim, tuple) else dim == 0
    return (fields, 1 if flat else tile[0], tile[1], tile[2])


def kernel(counts, perm, mean0, slopes, rocks, table, wcell, wrate, *rest):
    n_msg = len(ORDER)
    traces_o, flux_o, sat_o = rest[:3]
    sends = rest[3 : 3 + n_msg]
    recvs = rest[3 + n_msg : 3 + 2 * n_msg]
    phases = sum_phases(counts)
    n_sum = len(phases)
    sums = rest[3 + 2 * n_msg : 3 + 2 * n_msg + n_sum]
    send_sem, recv_sem, sum_send, sum_recv = rest[3 + 2 * n_msg + n_sum :]
    tile = mean0.shape
    tx, ty, tz = tile
    here = [lax.axis_index(a) for a in AXES]

    for m in range(n_msg):
        recvs[m][...] = jnp.zeros(recvs[m].shape, jnp.float32)

    barrier = pltpu.get_barrier_semaphore()
    partners = 0

    def peer_of(step):
        return {AXES[d]: lax.rem(here[d] + s, counts[d]) for d, s in step.items()}

    for dims in phases:
        for step in peers(dims, counts):
            pl.semaphore_signal(
                barrier, inc=1, device_id=peer_of(step), device_id_type=MESH
            )
            partners += 1

    def diagonal(d, e):
        return (here[d] > 0) & (here[e] < counts[e] - 1)

    for d, e in DIAGONALS if n_sum > 1 else ():

        @pl.when(diagonal(d, e))
        def _():
            pl.semaphore_signal(
                barrier,
                inc=1,
                device_id={AXES[d]: here[d] - 1, AXES[e]: here[e] + 1},
                device_id_type=MESH,
            )

    place = [lax.broadcasted_iota(jnp.int32, tile, d) for d in range(3)]
    first_edge = [place[d] == 0 for d in range(3)]
    last_edge = [place[d] == tile[d] - 1 for d in range(3)]

    def packed(m):
        dim, _, fields = ORDER[m]
        return is_packed(dim, fields, tile)

    def moves(m):
        dim, direction, _ = ORDER[m]
        if isinstance(dim, tuple):
            return [(dim[0], -1), (dim[1], 1)]
        return [(dim, direction)]

    def copy_of(m):
        return pltpu.make_async_remote_copy(
            src_ref=sends[m],
            dst_ref=recvs[m],
            send_sem=send_sem.at[m],
            recv_sem=recv_sem.at[m],
            device_id={AXES[a]: here[a] + step for a, step in moves(m)},
            device_id_type=MESH,
        )

    def reaches(a, step):
        return here[a] < counts[a] - 1 if step == 1 else here[a] > 0

    def sends_to(m):
        return functools.reduce(lambda p, q: p & q, [reaches(a, t) for a, t in moves(m)])

    def hears_from(m):
        return functools.reduce(lambda p, q: p & q, [reaches(a, -t) for a, t in moves(m)])

    def turned(field, dim, direction):
        if dim == 0:
            return field[tx - 1 : tx] if direction == 1 else field[0:1]
        return pltpu.roll(field, 1 if direction == 1 else tile[dim] - 1, dim)

    def launch_diagonal(k, d, e, field):
        m = NAMES["diag", k, d, e]
        sends[m][0] = turned(turned(field, e, 1), d, -1)

        @pl.when(sends_to(m))
        def _():
            copy_of(m).start()

    def land_diagonal(k, d, e):
        m = NAMES["diag", k, d, e]

        @pl.when(hears_from(m))
        def _():
            copy_of(m).wait_recv()

        return recvs[m][0]

    def launch(key, fields):
        m = NAMES[key]
        dim, direction, _ = ORDER[m]
        whole = fields
        kept = []
        planes = [(i, x) for i in range(len(fields)) for x in range(tx)]
        if packed(m):
            lane = place[2][0]
            pack = jnp.zeros((ty, tz), jnp.float32)
            for n, (i, x) in enumerate(planes):
                turn = n + 1 if direction == 1 else n
                part = fields[i][x]
                part = pltpu.roll(part, turn, 1) if turn else part
                pack = jnp.where(lane == n, part, pack)
            sends[m][0, 0] = pack
            fields = ()
            kept = None
        for i, field in enumerate(fields):
            if dim == 0:
                sends[m][i] = field[tx - 1 : tx] if direction == 1 else field[0:1]
                kept.append(field)
            else:
                turned = pltpu.roll(field, 1 if direction == 1 else tile[dim] - 1, dim)
                sends[m][i] = turned
                kept.append(turned)

        @pl.when(sends_to(m))
        def _():
            copy_of(m).start()

        if kept is None:
            turn = 1 if direction == 1 else tz - 1
            kept = [pltpu.roll(f, turn, 2) for f in whole]
        return kept

    def launch_all(key, fields):
        kept = [None] * 3
        for d in ROUTE:
            kept[d] = launch(key(d), fields(d))
        return kept

    def land_all(key, kept):
        got = [None] * 3
        for d in ARRIVAL:
            got[d] = land(key(d), kept[d])
        return got

    def land(key, kept):
        m = NAMES[key]
        dim, direction, _ = ORDER[m]

        @pl.when(hears_from(m))
        def _():
            copy_of(m).wait_recv()

        out = []
        if packed(m):
            pack = recvs[m][0, 0]
        for i, field in enumerate(kept):
            if packed(m):
                parts = []
                for x in range(tx):
                    n = i * tx + x
                    turn = (tz - n) % tz if direction == 1 else tz - 1 - n
                    parts.append(pltpu.roll(pack, turn, 1) if turn else pack)
                got = jnp.stack(parts)
            else:
                got = recvs[m][i]
            if dim == 0:
                if direction == 1:
                    parts = [got, field[: tx - 1]] if tx > 1 else [got]
                else:
                    parts = [field[1:], got] if tx > 1 else [got]
                out.append(jnp.concatenate(parts, 0))
            else:
                edge = first_edge[dim] if direction == 1 else last_edge[dim]
                out.append(jnp.where(edge, got, field))
        return out

    state = [mean0[...]] + [slopes[i] for i in range(slopes.shape[0])]

    def launch_state(s, st):
        kept = {}
        for d in (2, 0, 1):
            kept["up", d] = launch(("up", s, d), trace(st, d, 1.0))
            kept["down", d] = launch(("down", s, d), trace(st, d, -1.0))
        return kept

    ids = rocks[...]
    water = jnp.zeros(tile, jnp.float32)
    oil = jnp.zeros(tile, jnp.float32)
    for k in range(table.shape[1]):
        water = jnp.where(ids == k, table[0, k], water)
        oil = jnp.where(ids == k, table[1, k], oil)
    clipped = jnp.clip(state[0], 0.0, 1.0)
    mobility = water * clipped * clipped + oil * (1.0 - clipped) * (1.0 - clipped)
    conduct = [2.0 * perm[d] * mobility for d in range(3)]
    total = 2.0 * (conduct[0] + conduct[1] + conduct[2])
    inv_total = 1.0 / total
    third = inv_total * (1.0 / 3.0)
    half_inv = [0.5 / conduct[d] for d in range(3)]

    cell = (
        (here[0] * tx + place[0]) * (ty * counts[1]) + here[1] * ty + place[1]
    ) * (tz * counts[2]) + (here[2] * tz + place[2])
    n_wells = wcell.shape[0]
    group = int(np.gcd(n_wells, 16))

    def add_wells(g, acc):
        for i in range(group):
            w = g * group + i
            acc = acc + jnp.where(cell == wcell[w], wrate[w], 0)
        return acc

    source = 0.5 * lax.fori_loop(
        0, n_wells // group, add_wells, jnp.zeros(tile, jnp.int32)
    ).astype(jnp.float32)
    weighted = source * inv_total

    for d, e in DIAGONALS if n_sum > 1 else ():
        partners = partners + diagonal(d, e).astype(jnp.int32)
    pl.semaphore_wait(barrier, partners)
    kept = launch_all(lambda d: ("coef", d), lambda d: conduct + [weighted])
    prior_kept = launch_all(lambda d: ("prior", d), lambda d: [conduct[d], weighted])
    state_kept = launch_state(0, state)
    beyond, beyond_w, shares = [], [], []
    for d, got in enumerate(land_all(lambda d: ("coef", d), kept)):
        beyond.append(got[d])
        beyond_w.append(got[3])
        whole_sum = 2.0 * (got[0] + got[1] + got[2])
        inverse = 1.0 / jnp.where(whole_sum > 0.0, whole_sum, 1.0)
        shares.append([jnp.where(last_edge[d], got[e] * inverse, 0.0) for e in range(3)])
    for d, e in DIAGONALS:
        shares[d][e] = jnp.where(first_edge[e], shares[d][e], 0.0)

    def mean_of(v, prior):
        return (
            conduct[0] * (v[0] + prior[0])
            + conduct[1] * (v[1] + prior[1])
            + conduct[2] * (v[2] + prior[2])
        ) * inv_total

    def operator(k, v):
        for d, e in DIAGONALS:
            launch_diagonal(k, d, e, v[e])
        kept = launch_all(lambda d: ("vec", k, d), lambda d: [v[d]])
        inner = []
        for d in range(3):
            if d == 0:
                zero = jnp.zeros((1, ty, tz), jnp.float32)
                inner.append(jnp.concatenate([zero, v[0][: tx - 1]], 0) if tx > 1 else zero)
            else:
                inner.append(jnp.where(first_edge[d], 0.0, kept[d][0]))
        partial = mean_of(v, inner)
        launch_all(lambda d: ("mean", k, d), lambda d: [partial])
        prior = [got[0] for got in land_all(lambda d: ("vec", k, d), kept)]
        center = mean_of(v, prior)
        back = launch_all(lambda d: ("back", k, d), lambda d: [center])
        local = [conduct[d] * (v[d] - center) for d in range(3)]
        kept = [[center], [turned(center, 1, -1)], [turned(center, 2, -1)]]
        following = [got[0] for got in land_all(lambda d: ("mean", k, d), kept)]
        for d in range(3):
            following[d] = following[d] + shares[d][d] * v[d]
        for d, e in reversed(DIAGONALS):
            following[d] = following[d] + shares[d][e] * land_diagonal(k, d, e)
        image = [local[d] + beyond[d] * (v[d] - following[d]) for d in range(3)]
        return image, prior, center, following, back

    def precondition(r):
        shared = (r[0] + r[1] + r[2]) * third
        return [r[d] * half_inv[d] + shared for d in range(3)]

    def dot(a, b):
        both = jnp.sum(a[0] * b[0] + a[1] * b[1] + a[2] * b[2], axis=0)
        return jnp.sum(both, axis=0, keepdims=True)

    def place_in(dims):
        slot = 0
        for d in dims:
            slot = slot * counts[d] + here[d]
        return slot

    def send_sum(p, step):
        slot = place_in(phases[p])
        return pltpu.make_async_remote_copy(
            src_ref=sums[p].at[slot],
            dst_ref=sums[p].at[slot],
            send_sem=sum_send.at[p],
            recv_sem=sum_recv.at[p],
            device_id=peer_of(step),
            device_id_type=MESH,
        )

    def all_sums(p, sem):
        others_of = sums[p].at[pl.ds(0, sums[p].shape[0] - 1)]
        return pltpu.make_async_copy(others_of, others_of, sem.at[p])

    load = [
        conduct[d] * weighted
        + beyond[d] * beyond_w[d]
        + GRAVITY[d] * (beyond[d] - conduct[d])
        for d in range(3)
    ]
    basis, images, priors, centers, follows, backs = [], [], [], [], [], []
    vector = precondition(load)
    for k in range(ITERS):
        if k + 1 == ITERS:
            kept = launch_all(lambda d: ("vec", k, d), lambda d: [vector[d]])
            prior = [got[0] for got in land_all(lambda d: ("vec", k, d), kept)]
            center = mean_of(vector, prior)
            last_kept = launch_all(lambda d: ("mean", k, d), lambda d: [center])
            basis.append(vector)
            priors.append(prior)
            centers.append(center)
            break
        image, prior, center, following, back = operator(k, vector)
        basis.append(vector)
        images.append(image)
        priors.append(prior)
        centers.append(center)
        follows.append(following)
        backs.append(back)
        step = precondition(image)
        vector = [step[d] - SHIFT * vector[d] for d in range(3)]

    pairs = [(i, j) for i in range(ITERS) for j in range(i, ITERS)]
    rows = [dot(basis[j], images[i]) for i, j in pairs[:-1]]
    gaps = [vector[d] - center for d in range(3)] + [prior[d] - center for d in range(3)]
    rows.append(dot([conduct[d] * gaps[d] for d in range(3)], gaps[:3]))
    rows[-1] = rows[-1] + dot([conduct[d] * gaps[3 + d] for d in range(3)], gaps[3:])
    rows += [dot(basis[i], load) for i in range(ITERS)]
    acc = jnp.concatenate(rows + [jnp.zeros_like(rows[0])] * (-len(rows) % 8), 0)
    diag = lax.broadcasted_iota(jnp.int32, acc.shape, 0) == lax.broadcasted_iota(
        jnp.int32, acc.shape, 1
    )
    spread = acc.shape
    acc = jnp.where(diag, jnp.sum(acc, axis=1, keepdims=True), 0.0)
    acc = jnp.sum(acc, axis=0, keepdims=True)
    early = None
    backs.append(launch_all(lambda d: ("back", ITERS - 1, d), lambda d: [center]))
    for p, dims in enumerate(phases):
        sums[p][place_in(dims)] = acc
        for step in peers(dims, counts):
            send_sum(p, step).start()
        if early is None:
            early = cube_moments(state, water, oil)
        all_sums(p, sum_recv).wait()
        parts = [sums[p][j] for j in range(sums[p].shape[0])]
        while len(parts) > 1:
            parts = [sum(parts[j : j + 2]) for j in range(0, len(parts), 2)]
        acc = parts[0]
    full = jnp.where(diag, jnp.broadcast_to(acc, spread), 0.0)
    full = jnp.broadcast_to(jnp.sum(full, axis=1, keepdims=True), spread)
    gram = {}
    for r, (i, j) in enumerate(pairs):
        gram[i, j] = full[r : r + 1]
    right = [full[len(pairs) + i : len(pairs) + i + 1] for i in range(ITERS)]

    factor = {}
    for i in range(ITERS):
        for j in range(i + 1, ITERS):
            factor[j, i] = gram[i, j] / gram[i, i]
        for j in range(i + 1, ITERS):
            for m in range(j, ITERS):
                gram[j, m] = gram[j, m] - factor[j, i] * gram[i, m]
            right[j] = right[j] - factor[j, i] * right[i]
    coef = [None] * ITERS
    for i in reversed(range(ITERS)):
        value = right[i] / gram[i, i]
        for j in range(i + 1, ITERS):
            value = value - factor[j, i] * coef[j]
        coef[i] = value
    coef = [jnp.broadcast_to(c, (ty, tz))[None] for c in coef]

    def combine(parts):
        out = coef[0] * parts[0]
        for j in range(1, ITERS):
            out = out + coef[j] * parts[j]
        return out

    center = combine(centers)
    follows.append([got[0] for got in land_all(lambda d: ("mean", ITERS - 1, d), last_kept)])
    pressure = center + weighted
    prior_coef = land_all(lambda d: ("prior", d), prior_kept)
    fluxes, before = [None] * 3, [None] * 3
    for d in range(3):
        trace_d = combine([p[d] for p in basis])
        traces_o[d] = trace_d
        following = combine([f[d] for f in follows])
        fluxes[d] = 0.5 * (
            conduct[d] * (pressure - trace_d - GRAVITY[d])
            + beyond[d] * (trace_d - (following + beyond_w[d]) - GRAVITY[d])
        )
        flux_o[d] = fluxes[d]
        earlier = combine([p[d] for p in priors])
        back = combine([land(("back", k, d), backs[k][d])[0] for k in range(ITERS)])
        prior_k, prior_w = prior_coef[d]
        flux = 0.5 * (
            prior_k * ((back + prior_w) - earlier - GRAVITY[d])
            + conduct[d] * (earlier - pressure - GRAVITY[d])
        )
        before[d] = jnp.where(here[d] * tile[d] + place[d] == 0, 0.0, flux)
    after_pos = [fluxes[d] > 0.0 for d in range(3)]
    before_pos = [before[d] > 0.0 for d in range(3)]
    mid_speed = [0.5 * (before[d] + fluxes[d]) for d in range(3)]
    dif_speed = [0.5 * (fluxes[d] - before[d]) for d in range(3)]

    def rate(s, st, kept, cube=None):
        m1, mlin, msqr, mmix = cube or cube_moments(st, water, oil)
        out = [jnp.where(source > 0.0, source, source * frac(st[0], water, oil))] + [None] * 9
        for d in range(3):
            out[LIN[d]] = 2.0 * (mid_speed[d] * m1 + dif_speed[d] * mlin[d])
            out[SQR[d]] = 6.0 * (mid_speed[d] * mlin[d] + dif_speed[d] * msqr[d])
        for a, b in MIX:
            m = mmix[a, b]
            out[MIX[a, b]] = 2.0 * (
                mid_speed[a] * mlin[b]
                + dif_speed[a] * m
                + mid_speed[b] * mlin[a]
                + dif_speed[b] * m
            )
        for d in (1, 0, 2):
            e, f = others(d)
            upper = trace(st, d, 1.0)
            lower = trace(st, d, -1.0)
            prior = land(("up", s, d), kept["up", d])
            after = land(("down", s, d), kept["down", d])
            chosen = [jnp.where(after_pos[d], upper[t], after[t]) for t in range(6)]
            o = [fluxes[d] * m for m in square_moments(chosen, water, oil)]
            chosen = [jnp.where(before_pos[d], prior[t], lower[t]) for t in range(6)]
            i = [before[d] * m for m in square_moments(chosen, water, oil)]
            out[0] = out[0] + (i[0] - o[0])
            out[SQR[d]] = out[SQR[d]] + (i[0] - o[0])
            out[LIN[d]] = out[LIN[d]] - (i[0] + o[0])
            out[LIN[e]] = out[LIN[e]] + (i[1] - o[1])
            out[LIN[f]] = out[LIN[f]] + (i[2] - o[2])
            out[mix(d, e)] = out[mix(d, e)] - (i[1] + o[1])
            out[mix(d, f)] = out[mix(d, f)] - (i[2] + o[2])
            out[SQR[e]] = out[SQR[e]] + (i[3] - o[3])
            out[SQR[f]] = out[SQR[f]] + (i[4] - o[4])
            out[mix(e, f)] = out[mix(e, f)] + (i[5] - o[5])
        return [(STEP * MASS[m]) * out[m] for m in range(10)]

    change = rate(0, state, state_kept, early)
    first = [state[m] + change[m] for m in range(10)]
    change = rate(1, first, launch_state(1, first))
    second = [0.75 * state[m] + 0.25 * (first[m] + change[m]) for m in range(10)]
    change = rate(2, second, launch_state(2, second))
    for m in range(10):
        sat_o[m] = (1.0 / 3.0) * state[m] + (2.0 / 3.0) * (second[m] + change[m])

    for m in range(n_msg):

        @pl.when(sends_to(m))
        def _():
            copy_of(m).wait_send()

    for p in range(n_sum):
        all_sums(p, sum_send).wait()


def hand_on(a, b, c, a_out, b_out, c_out):
    a_out[...] = a[...]
    b_out[...] = b[...]
    c_out[...] = c[...]


def per_device(counts, perm, mean0, slopes, rocks, table, wcell, wrate):
    tile = mean0.shape
    f32 = jnp.float32
    bufs = [
        pltpu.VMEM(buffer_shape(dim, f, tile), f32) for dim, _, f in ORDER
    ]
    phases = sum_phases(counts)
    sums = [pltpu.VMEM((len(peers(p, counts)) + 1, 1, tile[2]), f32) for p in phases]
    vmem = pl.BlockSpec(memory_space=pltpu.VMEM)
    smem = pl.BlockSpec(memory_space=pltpu.SMEM)
    shapes = tuple(jax.ShapeDtypeStruct((n,) + tile, f32) for n in (3, 3, 10))
    results = pl.pallas_call(
        functools.partial(kernel, counts),
        out_shape=tuple(pltpu.VMEM(s.shape, f32) for s in shapes),
        in_specs=[vmem] * 4 + [smem] * 3,
        out_specs=(vmem,) * 3,
        scratch_shapes=bufs
        + bufs
        + sums
        + [pltpu.SemaphoreType.DMA((len(ORDER),))] * 2
        + [pltpu.SemaphoreType.DMA((max(1, len(phases)),))] * 2,
        compiler_params=pltpu.CompilerParams(collective_id=0, has_side_effects=True),
    )(perm, mean0, slopes, rocks, table, wcell, wrate)
    results = [pltpu.with_memory_space_constraint(r, pltpu.VMEM) for r in results]
    return pl.pallas_call(
        hand_on, out_shape=shapes, in_specs=[vmem] * 3, out_specs=(vmem,) * 3
    )(*results)


def solution(mesh):
    counts = tuple(mesh.shape[a] for a in AXES)
    grid = P(None, "gx", "gy", "gz")
    cells = P("gx", "gy", "gz")
    return jax.shard_map(
        functools.partial(per_device, counts),
        mesh=mesh,
        in_specs=(grid, cells, grid, cells, P(), P(), P()),
        out_specs=(grid, grid, grid),
        check_vma=False,
    )
```

```python
import functools
import itertools

import jax
import jax.numpy as jnp
import numpy as np
from jax import lax
from jax.experimental import pallas as pl
from jax.experimental.pallas import tpu as pltpu
from jax.sharding import PartitionSpec as P

ITERS = 3
STEP = 0.05
GRAVITY = (0.0, 0.0, 2.0)
SHIFT = 0.6
ROUTE = (2, 0, 1)
ARRIVAL = (1, 0, 2)
AXES = ("gx", "gy", "gz")
MESH = pl.DeviceIdType.MESH
ROOT = float(np.sqrt(0.6))
XI = (-ROOT, 0.0, ROOT)
LEG2 = (0.4, -0.5, 0.4)
WEIGHT = (5.0 / 18.0, 8.0 / 18.0, 5.0 / 18.0)

LIN = (1, 2, 3)
SQR = (4, 5, 6)
MIX = {(0, 1): 7, (0, 2): 8, (1, 2): 9}
MASS = (1.0, 3.0, 3.0, 3.0, 5.0, 5.0, 5.0, 9.0, 9.0, 9.0)


def mix(a, b):
    return MIX[(min(a, b), max(a, b))]


def others(d):
    return [e for e in range(3) if e != d]


HALO = ITERS
SLOT = 8


def message_list():
    names = {}
    order = []

    def add(key, dim, direction, fields):
        names[key] = len(order)
        order.append((dim, direction, fields))

    for d in range(3):
        add(("mean", d), d, -1, 1)
        add(("back", d), d, 1, 1)
    for s in range(3):
        for d in range(3):
            add(("up", s, d), d, 1, 6)
            add(("down", s, d), d, -1, 6)
    return names, order


NAMES, ORDER = message_list()
DIRECT = 64


def sum_phases(counts):
    split = [d for d in range(3) if counts[d] > 1]
    if int(np.prod(counts)) <= DIRECT:
        return [tuple(split)] if split else []
    return [(d,) for d in (1, 2, 0) if counts[d] > 1]


def peers(dims, counts):
    steps = itertools.product(*[range(counts[d]) for d in dims])
    return [dict(zip(dims, s)) for s in steps if any(s)]


def layers(m, tx):
    return tx if m == 0 else max(0, min(tx, HALO - (abs(m) - 1) * tx))


def halo_messages(counts, tx):
    reach = min(-(-HALO // tx), counts[0] - 1)
    rows = {1: (0,), 2: (0, "pair")}.get(counts[1], (0, 1, -1))
    columns = (0, 1, -1) if counts[2] > 1 else (0,)
    found = []
    for m in sorted(range(-reach, reach + 1), key=lambda m: -abs(m)):
        full = m != 0 and (abs(m) - 1) * tx + 1 >= HALO
        side = 1 if m > 0 else -1
        for c in columns:
            for r in rows:
                spare = full and side in (c, r)
                if not spare and (m, r, c) != (0, 0, 0):
                    found.append((m, r, c))
    return found


def pack_count(tile):
    return -(-3 * tile[0] // (tile[2] // SLOT))


def halo_shape(message, tile):
    m, _, c = message
    if c:
        return (pack_count(tile),) + tile[1:]
    return (layers(m, tile[0]), 3) + tile[1:]


class Slab:
    def __init__(self, lo, data):
        self.lo = lo
        self.data = data

    def get(self, lo, hi):
        return self.data[lo - self.lo : hi - self.lo]


def following_of(d, slab, lo, hi):
    if d == 0:
        return slab.get(lo + 1, hi + 1)
    part = slab.get(lo, hi)
    return pltpu.roll(part, part.shape[d] - 1, d)


def previous_of(d, slab, lo, hi):
    if d == 0:
        return slab.get(lo - 1, hi - 1)
    return pltpu.roll(slab.get(lo, hi), 1, d)


def invert(x):
    return pl.reciprocal(x, approx=True)


def frac(sat, water, oil):
    c = jnp.clip(sat, 0.0, 1.0)
    w = water * c * c
    r = 1.0 - c
    return w * pl.reciprocal(w + oil * r * r, approx=True)


def trace(state, d, sign):
    e, f = others(d)
    return [
        (state[0] + state[SQR[d]]) + sign * state[LIN[d]],
        state[LIN[e]] + sign * state[mix(d, e)],
        state[LIN[f]] + sign * state[mix(d, f)],
        state[SQR[e]],
        state[SQR[f]],
        state[mix(e, f)],
    ]


def square_moments(coefs, water, oil):
    base, s, t, ss, tt, st = coefs
    firsts, seconds, thirds = [], [], []
    for i in range(3):
        if i == 1:
            a = base + LEG2[1] * ss
            b = t
        else:
            a = base + XI[i] * s + LEG2[i] * ss
            b = t + XI[i] * st
        outer = a + LEG2[0] * tt
        lean = ROOT * b
        low = frac(outer - lean, water, oil)
        mid = frac(a + LEG2[1] * tt, water, oil)
        high = frac(outer + lean, water, oil)
        both = low + high
        firsts.append(WEIGHT[0] * both + WEIGHT[1] * mid)
        seconds.append((WEIGHT[0] * ROOT) * (high - low))
        thirds.append((WEIGHT[0] * LEG2[0]) * both + (WEIGHT[1] * LEG2[1]) * mid)
    ends = firsts[0] + firsts[2]
    m00 = WEIGHT[0] * ends + WEIGHT[1] * firsts[1]
    m10 = (WEIGHT[0] * ROOT) * (firsts[2] - firsts[0])
    m20 = (WEIGHT[0] * LEG2[0]) * ends + (WEIGHT[1] * LEG2[1]) * firsts[1]
    m01 = WEIGHT[0] * (seconds[0] + seconds[2]) + WEIGHT[1] * seconds[1]
    m11 = (WEIGHT[0] * ROOT) * (seconds[2] - seconds[0])
    m02 = WEIGHT[0] * (thirds[0] + thirds[2]) + WEIGHT[1] * thirds[1]
    return m00, m10, m01, m20, m02, m11


def cube_moments(state, water, oil):
    c0, cx, cy, cz, cxx, cyy, czz, cxy, cxz, cyz = state
    w, v, q = WEIGHT[0], WEIGHT[1], WEIGHT[0] * 0.6
    planes = []
    for i in range(3):
        if i == 1:
            a = c0 + LEG2[1] * cxx
            by, bz = cy, cz
        else:
            a = c0 + XI[i] * cx + LEG2[i] * cxx
            by = cy + XI[i] * cxy
            bz = cz + XI[i] * cxz
        rows = []
        for j in range(3):
            if j == 1:
                b = a + LEG2[1] * cyy
                g = bz
            else:
                b = a + XI[j] * by + LEG2[j] * cyy
                g = bz + XI[j] * cyz
            edge = b + LEG2[0] * czz
            lean = ROOT * g
            low = frac(edge - lean, water, oil)
            mid = frac(b + LEG2[1] * czz, water, oil)
            high = frac(edge + lean, water, oil)
            both = low + high
            rows.append((w * both + v * mid, (w * ROOT) * (high - low), q * both))
        r0, r1, r2 = zip(*rows)
        planes.append(
            (
                w * (r0[0] + r0[2]) + v * r0[1],
                (w * ROOT) * (r0[2] - r0[0]),
                q * (r0[0] + r0[2]),
                w * (r1[0] + r1[2]) + v * r1[1],
                (w * ROOT) * (r1[2] - r1[0]),
                w * (r2[0] + r2[2]) + v * r2[1],
            )
        )
    p00, p10, p20, p01, p11, p02 = zip(*planes)

    def even(p):
        return w * (p[0] + p[2]) + v * p[1]

    def odd(p):
        return (w * ROOT) * (p[2] - p[0])

    m1 = even(p00)
    mlin = (odd(p00), even(p10), even(p01))
    msqr = (q * (p00[0] + p00[2]), even(p20), even(p02))
    mmix = {(0, 1): odd(p10), (0, 2): odd(p01), (1, 2): even(p11)}
    return m1, mlin, msqr, mmix


def is_packed(dim, fields, tile):
    return dim == 2 and fields > 2 and fields * tile[0] < tile[2]


def buffer_shape(dim, fields, tile):
    if is_packed(dim, fields, tile):
        return (1, 1, tile[1], tile[2])
    return (fields, 1 if dim == 0 else tile[0], tile[1], tile[2])


def kernel(counts, messages, perm_h, mean_h, slopes_h, rocks_h, table_h, wcell_h, wrate_h, *rest):
    n_msg = len(ORDER)
    rest = list(rest)

    def take(n):
        part = rest[:n]
        del rest[:n]
        return part

    traces_o, flux_o, sat_o = take(3)
    sends, recvs = take(n_msg), take(n_msg)
    phases = sum_phases(counts)
    n_sum = len(phases)
    sums = take(n_sum)
    halos = dict(zip(messages, take(len(messages))))
    own_conduct, own_pack = take(2)
    perm, mean0, slopes, rocks, table, wcell, wrate = take(7)
    send_sem, recv_sem, sum_send, sum_recv, halo_send, halo_recv, in_sem = rest
    tile = mean0.shape
    tx, ty, tz = tile
    here = [lax.axis_index(a) for a in AXES]

    barrier = pltpu.get_barrier_semaphore()
    partners = 0

    def peer_of(step):
        return {AXES[d]: lax.rem(here[d] + s, counts[d]) for d, s in step.items()}

    for dims in phases:
        for step in peers(dims, counts):
            pl.semaphore_signal(
                barrier, inc=1, device_id=peer_of(step), device_id_type=MESH
            )
            partners += 1

    def inside(a, step):
        if step == 0:
            return []
        return [here[a] + step >= 0 if step < 0 else here[a] + step < counts[a]]

    def exists(message, sign):
        m, r, c = message
        r = 0 if r == "pair" else r
        return inside(0, sign * m) + inside(1, sign * r) + inside(2, sign * c)

    def target(message):
        m, r, c = message
        where = {}
        if m:
            where[AXES[0]] = here[0] - m
        if r:
            where[AXES[1]] = 1 - here[1] if r == "pair" else here[1] - r
        if c:
            where[AXES[2]] = here[2] - c
        return where

    if n_sum > 1:
        for message in messages:
            if sum(map(bool, message)) < 2:
                continue
            both = functools.reduce(lambda p, q: p & q, exists(message, -1), True)

            def greet():
                pl.semaphore_signal(
                    barrier, inc=1, device_id=target(message), device_id_type=MESH
                )

            if both is True:
                greet()
                partners += 1
            else:
                pl.when(both)(greet)
                partners = partners + both.astype(jnp.int32)

    inputs = [
        (rocks_h, rocks),
        (table_h, table),
        (mean_h, mean0),
        (perm_h, perm),
        (wcell_h, wcell),
        (wrate_h, wrate),
        (slopes_h, slopes),
    ]
    loads = [
        pltpu.make_async_copy(a, b, in_sem.at[i]) for i, (a, b) in enumerate(inputs)
    ]
    for copy in loads:
        copy.start()

    place = [lax.broadcasted_iota(jnp.int32, tile, d) for d in range(3)]
    first_edge = [place[d] == 0 for d in range(3)]
    last_edge = [place[d] == tile[d] - 1 for d in range(3)]

    def packed(m):
        dim, _, fields = ORDER[m]
        return is_packed(dim, fields, tile)

    def copy_of(m):
        dim, direction, _ = ORDER[m]
        return pltpu.make_async_remote_copy(
            src_ref=sends[m],
            dst_ref=recvs[m],
            send_sem=send_sem.at[m],
            recv_sem=recv_sem.at[m],
            device_id={AXES[dim]: here[dim] + direction},
            device_id_type=MESH,
        )

    def reaches(a, step):
        return here[a] < counts[a] - 1 if step == 1 else here[a] > 0

    def sends_to(m):
        return reaches(*ORDER[m][:2])

    def hears_from(m):
        return reaches(ORDER[m][0], -ORDER[m][1])

    def launch(key, fields):
        m = NAMES[key]
        dim, direction, _ = ORDER[m]
        whole = fields
        kept = []
        planes = [(i, x) for i in range(len(fields)) for x in range(tx)]
        if packed(m):
            lane = place[2][0]
            pack = jnp.zeros((ty, tz), jnp.float32)
            for n, (i, x) in enumerate(planes):
                turn = n + 1 if direction == 1 else n
                part = fields[i][x]
                part = pltpu.roll(part, turn, 1) if turn else part
                pack = jnp.where(lane == n, part, pack)
            sends[m][0, 0] = pack
            fields = ()
            kept = None
        for i, field in enumerate(fields):
            if dim == 0:
                sends[m][i] = field[tx - 1 : tx] if direction == 1 else field[0:1]
                kept.append(field)
            else:
                turned = pltpu.roll(field, 1 if direction == 1 else tile[dim] - 1, dim)
                sends[m][i] = turned
                kept.append(turned)

        @pl.when(sends_to(m))
        def _():
            copy_of(m).start()

        if kept is None:
            turn = 1 if direction == 1 else tz - 1
            kept = [pltpu.roll(f, turn, 2) for f in whole]
        return kept

    def launch_all(key, fields):
        kept = [None] * 3
        for d in ROUTE:
            kept[d] = launch(key(d), fields(d))
        return kept

    def land_all(key, kept):
        got = [None] * 3
        for d in ARRIVAL:
            got[d] = land(key(d), kept[d])
        return got

    def land(key, kept):
        m = NAMES[key]
        dim, direction, _ = ORDER[m]

        @pl.when(hears_from(m))
        def _():
            copy_of(m).wait_recv()

        @pl.when(jnp.logical_not(hears_from(m)))
        def _():
            recvs[m][...] = jnp.zeros(recvs[m].shape, jnp.float32)

        out = []
        if packed(m):
            pack = recvs[m][0, 0]
        for i, field in enumerate(kept):
            if packed(m):
                parts = []
                for x in range(tx):
                    n = i * tx + x
                    turn = (tz - n) % tz if direction == 1 else tz - 1 - n
                    parts.append(pltpu.roll(pack, turn, 1) if turn else pack)
                got = jnp.stack(parts)
            else:
                got = recvs[m][i]
            if dim == 0:
                if direction == 1:
                    parts = [got, field[: tx - 1]] if tx > 1 else [got]
                else:
                    parts = [field[1:], got] if tx > 1 else [got]
                out.append(jnp.concatenate(parts, 0))
            else:
                edge = first_edge[dim] if direction == 1 else last_edge[dim]
                out.append(jnp.where(edge, got, field))
        return out

    def launch_state(s, st):
        kept = {}
        for d in (2, 0, 1):
            kept["up", d] = launch(("up", s, d), trace(st, d, 1.0))
            kept["down", d] = launch(("down", s, d), trace(st, d, -1.0))
        return kept

    def halo_copy(message):
        m, _, c = message
        n = messages.index(message)
        if c:
            source = own_pack
        else:
            count = layers(m, tx)
            source = own_conduct.at[pl.ds(tx - count if m < 0 else 0, count)]
        return pltpu.make_async_remote_copy(
            src_ref=source,
            dst_ref=halos[message],
            send_sem=halo_send.at[n],
            recv_sem=halo_recv.at[n],
            device_id=target(message),
            device_id_type=MESH,
        )

    def each_halo(sign, act, missing=None):
        groups = {}
        for message in messages:
            m, r, c = message
            groups.setdefault((m, 0 if r == "pair" else r, c), []).append(message)
        for group in groups.values():
            conds = exists(group[0], sign)

            def run(act=act, group=group):
                for message in group:
                    act(message)

            if not conds:
                run()
                continue
            cond = functools.reduce(lambda p, q: p & q, conds)
            pl.when(cond)(run)
            if missing is not None:
                pl.when(jnp.logical_not(cond))(functools.partial(run, missing))

    for copy in loads[:4]:
        copy.wait()
    ids = rocks[...]
    water = jnp.zeros(tile, jnp.float32)
    oil = jnp.zeros(tile, jnp.float32)
    for k in range(table.shape[1]):
        water = jnp.where(ids == k, table[0, k], water)
        oil = jnp.where(ids == k, table[1, k], oil)
    mean_sat = mean0[...]
    clipped = jnp.clip(mean_sat, 0.0, 1.0)
    mobility = water * clipped * clipped + oil * (1.0 - clipped) * (1.0 - clipped)
    conduct = [2.0 * perm[d] * mobility for d in range(3)]
    per = tz // SLOT
    row2 = place[1][0]
    lane2 = place[2][0]
    slot_of = lax.rem(lane2 + SLOT // 2, tz) // SLOT
    packs = [jnp.zeros((ty, tz), jnp.float32) for _ in range(pack_count(tile))]
    for x in range(tx):
        for f in range(3):
            own_conduct[x, f] = conduct[f][x]
            p, n = divmod(x * 3 + f, per)
            part = conduct[f][x]
            part = pltpu.roll(part, n * SLOT, 1) if n else part
            packs[p] = jnp.where(slot_of == n, part, packs[p])
    for p, pack in enumerate(packs):
        own_pack[p] = pack

    pl.semaphore_wait(barrier, partners)
    each_halo(-1, lambda message: halo_copy(message).start())

    for copy in loads[4:]:
        copy.wait()
    state = [mean_sat] + [slopes[i] for i in range(slopes.shape[0])]
    state_kept = launch_state(0, state)

    lo, hi = -HALO, tx + HALO
    ring = (hi - lo, 2 * ty, 2 * tz)

    def position(index, size):
        return jnp.where(index < size + size // 2, index, index - 2 * size)

    n_wells = wcell.shape[1]
    nz = tz * counts[2]
    cells = wcell[...]
    line = ((cells.astype(jnp.float32) + 0.5) * (1.0 / nz)).astype(jnp.int32)
    column = cells - line * nz
    half_rates = 0.5 * wrate[...].astype(jnp.float32)
    plane_at = lax.broadcasted_iota(jnp.int32, ring[:2] + (n_wells,), 0)
    row_at = lax.broadcasted_iota(jnp.int32, ring[:2] + (n_wells,), 1)
    line_at = (here[0] * tx + lo + plane_at) * (ty * counts[1]) + (
        here[1] * ty + position(row_at, ty)
    )
    column_at = here[2] * tz + position(
        lax.broadcasted_iota(jnp.int32, (2 * tz, n_wells), 0), tz
    )
    by_line = jnp.where(line_at == line[None], half_rates[None], 0.0)
    by_line = by_line.reshape(ring[0] * ring[1], n_wells).astype(jnp.bfloat16)
    by_column = jnp.where(column_at == column, 1.0, 0.0).astype(jnp.bfloat16)
    sources = lax.dot_general(
        by_line,
        by_column,
        (((1,), (1,)), ((), ())),
        preferred_element_type=jnp.float32,
    ).reshape(ring)

    def clear(message):
        halos[message][...] = jnp.zeros(halos[message].shape, jnp.float32)

    each_halo(1, lambda message: halo_copy(message).wait_recv(), clear)

    blank = jnp.zeros((ty, tz), jnp.float32)
    from_next = lax.rem(lane2, SLOT) < SLOT // 2
    upper_rows = row2 < ty // 2
    pair_rows = jnp.where(here[1] == 0, row2, ty - 1 - row2) < ty // 2

    def rows_beyond(get):
        if counts[1] == 1:
            return blank
        if counts[1] == 2:
            return jnp.where(pair_rows, get("pair"), 0.0)
        return jnp.where(upper_rows, get(1), get(-1))

    def whole_tile(m, r, x, f):
        if (m, r) == (0, 0):
            return conduct[f][x]
        if (m, r, 0) not in halos:
            return blank
        first = tx - layers(m, tx) if m < 0 else 0
        return halos[m, r, 0][x - first, f]

    def pack_tile(m, r, p):
        sides = [
            halos[m, r, c][p] if (m, r, c) in halos else blank for c in (1, -1)
        ]
        return jnp.where(from_next, *sides)

    merged = {}

    def side_tile(m, beyond, x, f):
        p, n = divmod(x * 3 + f, per)
        if (m, beyond, p) not in merged:
            get = functools.partial(lambda r: pack_tile(m, r, p))
            merged[m, beyond, p] = rows_beyond(get) if beyond else get(0)
        tile2 = merged[m, beyond, p]
        return pltpu.roll(tile2, tz - n * SLOT, 1) if n else tile2

    def ring_plane(p, f):
        m, x = divmod(p, tx)
        near = [whole_tile(m, 0, x, f), side_tile(m, False, x, f)]
        far = [rows_beyond(lambda r: whole_tile(m, r, x, f)), side_tile(m, True, x, f)]
        return jnp.concatenate(
            [jnp.concatenate(near, 1), jnp.concatenate(far, 1)], 0
        )

    cond = [
        Slab(lo, jnp.stack([ring_plane(p, f) for p in range(lo, hi)])) for f in range(3)
    ]
    full = 2.0 * (cond[0].data + cond[1].data + cond[2].data)
    inv_total = Slab(lo, jnp.where(full > 0.0, invert(full), 0.0))
    weighted = Slab(lo, sources * inv_total.data)
    third = Slab(lo, inv_total.data * (1.0 / 3.0))
    half_inv = [
        Slab(lo, jnp.where(c.data > 0.0, 0.5 * invert(c.data), 0.0)) for c in cond
    ]

    def own(data, at=0):
        return data[at : at + tx, :ty, :tz]

    def own_of(slab):
        return own(slab.data, -slab.lo)

    def precondition(r, lo, hi):
        shared = (r[0] + r[1] + r[2]) * third.get(lo, hi)
        return [Slab(lo, r[d] * half_inv[d].get(lo, hi) + shared) for d in range(3)]

    hi -= 1
    load = []
    for d in range(3):
        lift = weighted.data + GRAVITY[d] if GRAVITY[d] else weighted.data
        drop = weighted.data - GRAVITY[d] if GRAVITY[d] else weighted.data
        after = following_of(d, Slab(-HALO, cond[d].data * lift), lo, hi)
        load.append(cond[d].get(lo, hi) * drop[: hi - lo] + after)
    vector = precondition(load, lo, hi)
    load = [own(r, -lo) for r in load]
    both = [
        Slab(lo + 1, cond[d].get(lo + 1, hi - 1) + following_of(d, cond[d], lo + 1, hi - 1))
        for d in range(3)
    ]
    basis, images, priors, means = [], [], [], []
    for k in range(ITERS):
        lo += 1
        previous = [previous_of(d, vector[d], lo, hi) for d in range(3)]
        total = sum(
            cond[d].get(lo, hi) * (vector[d].get(lo, hi) + previous[d]) for d in range(3)
        )
        mean = Slab(lo, total * inv_total.get(lo, hi))
        basis.append([own_of(v) for v in vector])
        priors.append([own(p, -lo) for p in previous])
        means.append(mean)
        if k + 1 == ITERS:
            break
        hi -= 1
        image = []
        for d in range(3):
            spread = Slab(lo, cond[d].get(lo, hi + 1) * mean.data)
            image.append(
                both[d].get(lo, hi) * vector[d].get(lo, hi)
                - (spread.get(lo, hi) + following_of(d, spread, lo, hi))
            )
        images.append([own(g, -lo) for g in image])
        fresh = precondition(image, lo, hi)
        vector = [
            Slab(lo, fresh[d].data - SHIFT * vector[d].get(lo, hi)) for d in range(3)
        ]
    center = own_of(means[-1])

    def dot(a, b):
        both = jnp.sum(a[0] * b[0] + a[1] * b[1] + a[2] * b[2], axis=0)
        return jnp.sum(both, axis=0, keepdims=True)

    def place_in(dims):
        slot = 0
        for d in dims:
            slot = slot * counts[d] + here[d]
        return slot

    def send_sum(p, step):
        slot = place_in(phases[p])
        return pltpu.make_async_remote_copy(
            src_ref=sums[p].at[slot],
            dst_ref=sums[p].at[slot],
            send_sem=sum_send.at[p],
            recv_sem=sum_recv.at[p],
            device_id=peer_of(step),
            device_id_type=MESH,
        )

    def all_sums(p, sem):
        others_of = sums[p].at[pl.ds(0, sums[p].shape[0] - 1)]
        return pltpu.make_async_copy(others_of, others_of, sem.at[p])

    at_start = [here[d] * tile[d] + place[d] == 0 for d in range(3)]

    def flux_parts(d, m, m_next, m_back, v, v_back):
        after = conduct[d] * (m - v) + beyond[d] * (v - m_next)
        prior = prior_c[d] * (m_back - v_back) + conduct[d] * (v_back - m)
        return 0.5 * after, jnp.where(at_start[d], 0.0, 0.5 * prior)

    def neighbours(slab):
        after = [own(following_of(d, slab, 0, tx)) for d in range(3)]
        prior = [own(previous_of(d, slab, 0, tx)) for d in range(3)]
        return after, prior

    beyond = [own(following_of(d, cond[d], 0, tx)) for d in range(3)]
    prior_c = [own(previous_of(d, cond[d], 0, tx)) for d in range(3)]

    def prepare():
        ahead = launch_all(lambda d: ("mean", d), lambda d: [center])
        behind = launch_all(lambda d: ("back", d), lambda d: [center])
        cube = cube_moments(state, water, oil)
        faces = stage_faces(0, state, state_kept)
        moments = cube, [[square_moments(f, water, oil) for f in four] for four in faces]
        each_halo(-1, lambda message: halo_copy(message).wait_send())
        parts = [[None] * (ITERS + 1) for _ in range(3)]
        w_next, w_back = neighbours(weighted)
        w = own_of(weighted)
        for d in range(3):
            g = GRAVITY[d]
            after = conduct[d] * (w - g) - beyond[d] * (w_next[d] + g)
            prior = prior_c[d] * (w_back[d] - g) - conduct[d] * (w + g)
            parts[d][ITERS] = 0.5 * after, jnp.where(at_start[d], 0.0, 0.5 * prior)
        for k in range(ITERS):
            if k + 1 < ITERS:
                m_next, m_back = neighbours(means[k])
            else:
                m_next = [got[0] for got in land_all(lambda d: ("mean", d), ahead)]
                m_back = [got[0] for got in land_all(lambda d: ("back", d), behind)]
            m = own_of(means[k])
            for d in range(3):
                parts[d][k] = flux_parts(
                    d, m, m_next[d], m_back[d], basis[k][d], priors[k][d]
                )
        return parts, moments

    def stage_faces(s, st, kept):
        faces = [None] * 3
        for d in (1, 0, 2):
            faces[d] = (
                trace(st, d, 1.0),
                land(("down", s, d), kept["down", d]),
                land(("up", s, d), kept["up", d]),
                trace(st, d, -1.0),
            )
        return faces

    source = own(sources, HALO)

    pairs = [(i, j) for i in range(ITERS) for j in range(i, ITERS)]
    rows = [dot(basis[j], images[i]) for i, j in pairs[:-1]]
    gaps = [part - center for part in basis[-1] + priors[-1]]
    rows.append(dot([conduct[d] * gaps[d] for d in range(3)], gaps[:3]))
    rows[-1] = rows[-1] + dot([conduct[d] * gaps[3 + d] for d in range(3)], gaps[3:])
    rows += [dot(basis[i], load) for i in range(ITERS)]
    acc = jnp.concatenate(rows + [jnp.zeros_like(rows[0])] * (-len(rows) % 8), 0)
    diag = lax.broadcasted_iota(jnp.int32, acc.shape, 0) == lax.broadcasted_iota(
        jnp.int32, acc.shape, 1
    )
    spread = acc.shape
    acc = jnp.where(diag, jnp.sum(acc, axis=1, keepdims=True), 0.0)
    acc = jnp.sum(acc, axis=0, keepdims=True)
    early = None
    for p, dims in enumerate(phases):
        sums[p][place_in(dims)] = acc
        for step in peers(dims, counts):
            send_sum(p, step).start()
        if early is None:
            early = prepare()
        all_sums(p, sum_recv).wait()
        parts = [sums[p][j] for j in range(sums[p].shape[0])]
        while len(parts) > 1:
            parts = [sum(parts[j : j + 2]) for j in range(0, len(parts), 2)]
        acc = parts[0]
    early = early or prepare()
    parts, moments = early
    full = jnp.where(diag, jnp.broadcast_to(acc, spread), 0.0)
    full = jnp.broadcast_to(jnp.sum(full, axis=1, keepdims=True), spread)
    gram = {}
    for r, (i, j) in enumerate(pairs):
        gram[i, j] = full[r : r + 1]
    right = [full[len(pairs) + i : len(pairs) + i + 1] for i in range(ITERS)]

    factor = {}
    for i in range(ITERS):
        for j in range(i + 1, ITERS):
            factor[j, i] = gram[i, j] / gram[i, i]
        for j in range(i + 1, ITERS):
            for m in range(j, ITERS):
                gram[j, m] = gram[j, m] - factor[j, i] * gram[i, m]
            right[j] = right[j] - factor[j, i] * right[i]
    coef = [None] * ITERS
    for i in reversed(range(ITERS)):
        value = right[i] / gram[i, i]
        for j in range(i + 1, ITERS):
            value = value - factor[j, i] * coef[j]
        coef[i] = value
    coef = [jnp.broadcast_to(c, (ty, tz))[None] for c in coef]

    def combine(parts):
        out = coef[0] * parts[0]
        for j in range(1, ITERS):
            out = out + coef[j] * parts[j]
        return out

    fluxes, before = [None] * 3, [None] * 3
    for d in range(3):
        traces_o[d] = combine([p[d] for p in basis])
        fluxes[d] = combine([p[0] for p in parts[d][:ITERS]]) + parts[d][ITERS][0]
        before[d] = combine([p[1] for p in parts[d][:ITERS]]) + parts[d][ITERS][1]
        flux_o[d] = fluxes[d]
    after_pos = [fluxes[d] > 0.0 for d in range(3)]
    before_pos = [before[d] > 0.0 for d in range(3)]
    mid_speed = [0.5 * (before[d] + fluxes[d]) for d in range(3)]
    dif_speed = [0.5 * (fluxes[d] - before[d]) for d in range(3)]

    def rate(s, st, kept=None, moments=None):
        if moments is None:
            cube = cube_moments(st, water, oil)
            faces = stage_faces(s, st, kept)
        else:
            cube, squares = moments
        m1, mlin, msqr, mmix = cube
        out = [jnp.where(source > 0.0, source, source * frac(st[0], water, oil))] + [None] * 9
        for d in range(3):
            out[LIN[d]] = 2.0 * (mid_speed[d] * m1 + dif_speed[d] * mlin[d])
            out[SQR[d]] = 6.0 * (mid_speed[d] * mlin[d] + dif_speed[d] * msqr[d])
        for a, b in MIX:
            m = mmix[a, b]
            out[MIX[a, b]] = 2.0 * (
                mid_speed[a] * mlin[b]
                + dif_speed[a] * m
                + mid_speed[b] * mlin[a]
                + dif_speed[b] * m
            )
        for d in (1, 0, 2):
            e, f = others(d)
            pick = lambda flag, a, b: [jnp.where(flag, p, q) for p, q in zip(a, b)]
            if moments is None:
                upper, after, prior, lower = faces[d]
                o = square_moments(pick(after_pos[d], upper, after), water, oil)
                i = square_moments(pick(before_pos[d], prior, lower), water, oil)
            else:
                upper, after, prior, lower = squares[d]
                o = pick(after_pos[d], upper, after)
                i = pick(before_pos[d], prior, lower)
            o = [fluxes[d] * m for m in o]
            i = [before[d] * m for m in i]
            out[0] = out[0] + (i[0] - o[0])
            out[SQR[d]] = out[SQR[d]] + (i[0] - o[0])
            out[LIN[d]] = out[LIN[d]] - (i[0] + o[0])
            out[LIN[e]] = out[LIN[e]] + (i[1] - o[1])
            out[LIN[f]] = out[LIN[f]] + (i[2] - o[2])
            out[mix(d, e)] = out[mix(d, e)] - (i[1] + o[1])
            out[mix(d, f)] = out[mix(d, f)] - (i[2] + o[2])
            out[SQR[e]] = out[SQR[e]] + (i[3] - o[3])
            out[SQR[f]] = out[SQR[f]] + (i[4] - o[4])
            out[mix(e, f)] = out[mix(e, f)] + (i[5] - o[5])
        return [(STEP * MASS[m]) * out[m] for m in range(10)]

    change = rate(0, state, moments=moments)
    first = [state[m] + change[m] for m in range(10)]
    change = rate(1, first, launch_state(1, first))
    second = [0.75 * state[m] + 0.25 * (first[m] + change[m]) for m in range(10)]
    change = rate(2, second, launch_state(2, second))
    for m in range(10):
        sat_o[m] = (1.0 / 3.0) * state[m] + (2.0 / 3.0) * (second[m] + change[m])

    for m in range(n_msg):

        @pl.when(sends_to(m))
        def _():
            copy_of(m).wait_send()

    for p in range(n_sum):
        all_sums(p, sum_send).wait()


def hand_on(a, b, c, a_out, b_out, c_out):
    a_out[...] = a[...]
    b_out[...] = b[...]
    c_out[...] = c[...]


def per_device(counts, perm, mean0, slopes, rocks, table, wcell, wrate):
    tile = mean0.shape
    f32 = jnp.float32
    bufs = [
        pltpu.VMEM(buffer_shape(dim, f, tile), f32) for dim, _, f in ORDER
    ]
    phases = sum_phases(counts)
    sums = [pltpu.VMEM((len(peers(p, counts)) + 1, 1, tile[2]), f32) for p in phases]
    messages = halo_messages(counts, tile[0])
    halos = [pltpu.VMEM(halo_shape(m, tile), f32) for m in messages]
    own_halo = [
        pltpu.VMEM((tile[0], 3) + tile[1:], f32),
        pltpu.VMEM((pack_count(tile),) + tile[1:], f32),
    ]
    wcell, wrate = wcell.reshape(1, -1), wrate.reshape(1, -1)
    operands = (perm, mean0, slopes, rocks, table, wcell, wrate)
    copies = [
        (pltpu.SMEM if a is table else pltpu.VMEM)(a.shape, a.dtype) for a in operands
    ]
    vmem = pl.BlockSpec(memory_space=pltpu.VMEM)
    hbm = pl.BlockSpec(memory_space=pltpu.HBM)
    dma = pltpu.SemaphoreType.DMA
    shapes = tuple(jax.ShapeDtypeStruct((n,) + tile, f32) for n in (3, 3, 10))
    results = pl.pallas_call(
        functools.partial(kernel, counts, messages),
        out_shape=tuple(pltpu.VMEM(s.shape, f32) for s in shapes),
        in_specs=[hbm] * len(operands),
        out_specs=(vmem,) * 3,
        scratch_shapes=bufs
        + bufs
        + sums
        + halos
        + own_halo
        + copies
        + [dma((len(ORDER),))] * 2
        + [dma((max(1, len(phases)),))] * 2
        + [dma((len(messages),))] * 2
        + [dma((len(operands),))],
        compiler_params=pltpu.CompilerParams(collective_id=0, has_side_effects=True),
    )(*operands)
    results = [pltpu.with_memory_space_constraint(r, pltpu.VMEM) for r in results]
    return pl.pallas_call(
        hand_on, out_shape=shapes, in_specs=[vmem] * 3, out_specs=(vmem,) * 3
    )(*results)


def solution(mesh):
    counts = tuple(mesh.shape[a] for a in AXES)
    grid = P(None, "gx", "gy", "gz")
    cells = P("gx", "gy", "gz")
    return jax.shard_map(
        functools.partial(per_device, counts),
        mesh=mesh,
        in_specs=(grid, cells, grid, cells, P(), P(), P()),
        out_specs=(grid, grid, grid),
        check_vma=False,
    )
```

```python
import functools
import itertools

import jax
import jax.numpy as jnp
import numpy as np
from jax import lax
from jax.experimental import pallas as pl
from jax.experimental.pallas import tpu as pltpu
from jax.sharding import PartitionSpec as P

ITERS = 3
STEP = 0.05
GRAVITY = (0.0, 0.0, 2.0)
SHIFT = 0.6
ROUTE = (2, 0, 1)
ARRIVAL = (1, 0, 2)
AXES = ("gx", "gy", "gz")
MESH = pl.DeviceIdType.MESH
ROOT = float(np.sqrt(0.6))
XI = (-ROOT, 0.0, ROOT)
LEG2 = (0.4, -0.5, 0.4)
WEIGHT = (5.0 / 18.0, 8.0 / 18.0, 5.0 / 18.0)

LIN = (1, 2, 3)
SQR = (4, 5, 6)
MIX = {(0, 1): 7, (0, 2): 8, (1, 2): 9}
MASS = (1.0, 3.0, 3.0, 3.0, 5.0, 5.0, 5.0, 9.0, 9.0, 9.0)


def mix(a, b):
    return MIX[(min(a, b), max(a, b))]


def others(d):
    return [e for e in range(3) if e != d]


HALO = ITERS
SLOT = 8


def message_list():
    names = {}
    order = []

    def add(key, dim, direction, fields):
        names[key] = len(order)
        order.append((dim, direction, fields))

    for d in range(3):
        add(("mean", d), d, -1, 1)
        add(("back", d), d, 1, 1)
    for s in range(3):
        for d in range(3):
            add(("up", s, d), d, 1, 6)
            add(("down", s, d), d, -1, 6)
    return names, order


NAMES, ORDER = message_list()
DIRECT = 64


def sum_phases(counts):
    split = [d for d in range(3) if counts[d] > 1]
    if int(np.prod(counts)) <= DIRECT:
        return [tuple(split)] if split else []
    return [(d,) for d in (1, 2, 0) if counts[d] > 1]


def peers(dims, counts):
    steps = itertools.product(*[range(counts[d]) for d in dims])
    return [dict(zip(dims, s)) for s in steps if any(s)]


def layers(m, tx):
    return tx if m == 0 else max(0, min(tx, HALO - (abs(m) - 1) * tx))


def halo_messages(counts, tx):
    reach = min(-(-HALO // tx), counts[0] - 1)
    rows = {1: (0,), 2: (0, "pair")}.get(counts[1], (0, 1, -1))
    columns = (0, 1, -1) if counts[2] > 1 else (0,)
    found = []
    for m in sorted(range(-reach, reach + 1), key=lambda m: -abs(m)):
        full = m != 0 and (abs(m) - 1) * tx + 1 >= HALO
        side = 1 if m > 0 else -1
        for c in columns:
            for r in rows:
                spare = full and side in (c, r)
                if not spare and (m, r, c) != (0, 0, 0):
                    found.append((m, r, c))
    return found


def pack_count(tile):
    return -(-3 * tile[0] // (tile[2] // SLOT))


def halo_part(message, tile):
    m, r, c = message
    count = layers(m, tile[0])
    first = tile[0] - count if m < 0 else 0
    if c == 0:
        return ("half" if r == "pair" else "whole", first, count)
    if r == "pair":
        return ("half strips",)
    folds = r == 0 and 6 * tile[0] * SLOT <= tile[2]
    return ("folded strips",) if folds else ("strips",)


def part_shape(part, tile):
    tx, ty, tz = tile
    if part[0] == "whole":
        return (part[2], 3, ty, tz)
    if part[0] == "half":
        return ((3 * part[2] + 1) // 2, ty, tz)
    return (pack_count(tile), ty if part[0] == "strips" else ty // 2, tz)


class Slab:
    def __init__(self, lo, data):
        self.lo = lo
        self.data = data

    def get(self, lo, hi):
        return self.data[lo - self.lo : hi - self.lo]


def following_of(d, slab, lo, hi):
    if d == 0:
        return slab.get(lo + 1, hi + 1)
    part = slab.get(lo, hi)
    return pltpu.roll(part, part.shape[d] - 1, d)


def previous_of(d, slab, lo, hi):
    if d == 0:
        return slab.get(lo - 1, hi - 1)
    return pltpu.roll(slab.get(lo, hi), 1, d)


def invert(x):
    return pl.reciprocal(x, approx=True)


def frac(sat, water, oil):
    c = jnp.clip(sat, 0.0, 1.0)
    w = water * c * c
    r = 1.0 - c
    return w * pl.reciprocal(w + oil * r * r, approx=True)


def trace(state, d, sign):
    e, f = others(d)
    return [
        (state[0] + state[SQR[d]]) + sign * state[LIN[d]],
        state[LIN[e]] + sign * state[mix(d, e)],
        state[LIN[f]] + sign * state[mix(d, f)],
        state[SQR[e]],
        state[SQR[f]],
        state[mix(e, f)],
    ]


def square_moments(coefs, water, oil):
    base, s, t, ss, tt, st = coefs
    firsts, seconds, thirds = [], [], []
    for i in range(3):
        if i == 1:
            a = base + LEG2[1] * ss
            b = t
        else:
            a = base + XI[i] * s + LEG2[i] * ss
            b = t + XI[i] * st
        outer = a + LEG2[0] * tt
        lean = ROOT * b
        low = frac(outer - lean, water, oil)
        mid = frac(a + LEG2[1] * tt, water, oil)
        high = frac(outer + lean, water, oil)
        both = low + high
        firsts.append(WEIGHT[0] * both + WEIGHT[1] * mid)
        seconds.append((WEIGHT[0] * ROOT) * (high - low))
        thirds.append((WEIGHT[0] * LEG2[0]) * both + (WEIGHT[1] * LEG2[1]) * mid)
    ends = firsts[0] + firsts[2]
    m00 = WEIGHT[0] * ends + WEIGHT[1] * firsts[1]
    m10 = (WEIGHT[0] * ROOT) * (firsts[2] - firsts[0])
    m20 = (WEIGHT[0] * LEG2[0]) * ends + (WEIGHT[1] * LEG2[1]) * firsts[1]
    m01 = WEIGHT[0] * (seconds[0] + seconds[2]) + WEIGHT[1] * seconds[1]
    m11 = (WEIGHT[0] * ROOT) * (seconds[2] - seconds[0])
    m02 = WEIGHT[0] * (thirds[0] + thirds[2]) + WEIGHT[1] * thirds[1]
    return m00, m10, m01, m20, m02, m11


def cube_moments(state, water, oil):
    c0, cx, cy, cz, cxx, cyy, czz, cxy, cxz, cyz = state
    w, v, q = WEIGHT[0], WEIGHT[1], WEIGHT[0] * 0.6
    planes = []
    for i in range(3):
        if i == 1:
            a = c0 + LEG2[1] * cxx
            by, bz = cy, cz
        else:
            a = c0 + XI[i] * cx + LEG2[i] * cxx
            by = cy + XI[i] * cxy
            bz = cz + XI[i] * cxz
        rows = []
        for j in range(3):
            if j == 1:
                b = a + LEG2[1] * cyy
                g = bz
            else:
                b = a + XI[j] * by + LEG2[j] * cyy
                g = bz + XI[j] * cyz
            edge = b + LEG2[0] * czz
            lean = ROOT * g
            low = frac(edge - lean, water, oil)
            mid = frac(b + LEG2[1] * czz, water, oil)
            high = frac(edge + lean, water, oil)
            both = low + high
            rows.append((w * both + v * mid, (w * ROOT) * (high - low), q * both))
        r0, r1, r2 = zip(*rows)
        planes.append(
            (
                w * (r0[0] + r0[2]) + v * r0[1],
                (w * ROOT) * (r0[2] - r0[0]),
                q * (r0[0] + r0[2]),
                w * (r1[0] + r1[2]) + v * r1[1],
                (w * ROOT) * (r1[2] - r1[0]),
                w * (r2[0] + r2[2]) + v * r2[1],
            )
        )
    p00, p10, p20, p01, p11, p02 = zip(*planes)

    def even(p):
        return w * (p[0] + p[2]) + v * p[1]

    def odd(p):
        return (w * ROOT) * (p[2] - p[0])

    m1 = even(p00)
    mlin = (odd(p00), even(p10), even(p01))
    msqr = (q * (p00[0] + p00[2]), even(p20), even(p02))
    mmix = {(0, 1): odd(p10), (0, 2): odd(p01), (1, 2): even(p11)}
    return m1, mlin, msqr, mmix


def is_packed(dim, fields, tile):
    return dim == 2 and fields > 2 and fields * tile[0] < tile[2]


def buffer_shape(dim, fields, tile):
    if is_packed(dim, fields, tile):
        return (1, 1, tile[1], tile[2])
    return (fields, 1 if dim == 0 else tile[0], tile[1], tile[2])


def kernel(counts, messages, perm_h, mean_h, slopes_h, rocks_h, table_h, wcell_h, wrate_h, *rest):
    n_msg = len(ORDER)
    rest = list(rest)

    def take(n):
        part = rest[:n]
        del rest[:n]
        return part

    traces_o, flux_o, sat_o = take(3)
    sends, recvs = take(n_msg), take(n_msg)
    phases = sum_phases(counts)
    n_sum = len(phases)
    sums = take(n_sum)
    halos = dict(zip(messages, take(len(messages))))
    parts_of = {message: halo_part(message, mean_h.shape) for message in messages}
    made = sorted({p for p in parts_of.values() if p[0] != "whole"})
    own_conduct = take(1)[0]
    own_parts = dict(zip(made, take(len(made))))
    perm, mean0, slopes, rocks, table, wcell, wrate = take(7)
    send_sem, recv_sem, sum_send, sum_recv, halo_send, halo_recv, in_sem = rest
    tile = mean0.shape
    tx, ty, tz = tile
    here = [lax.axis_index(a) for a in AXES]

    barrier = pltpu.get_barrier_semaphore()
    partners = 0

    def nearness(step):
        return sum(min(s, counts[d] - s) for d, s in step.items())

    def farness(step):
        return -sum(counts[d] - s for d, s in step.items() if s)

    def peer_of(step):
        return {AXES[d]: lax.rem(here[d] + s, counts[d]) for d, s in step.items()}

    for dims in phases:
        for step in sorted(peers(dims, counts), key=nearness):
            pl.semaphore_signal(
                barrier, inc=1, device_id=peer_of(step), device_id_type=MESH
            )
            partners += 1

    def inside(a, step):
        if step == 0:
            return []
        return [here[a] + step >= 0 if step < 0 else here[a] + step < counts[a]]

    def exists(message, sign):
        m, r, c = message
        found = inside(0, sign * m) + inside(2, sign * c)
        if r != "pair":
            return found + inside(1, sign * r)
        if m and (abs(m) - 1) * mean_h.shape[0] + 1 >= HALO:
            found.append(here[1] == int((m > 0) == (sign > 0)))
        return found

    def target(message):
        m, r, c = message
        where = {}
        if m:
            where[AXES[0]] = here[0] - m
        if r:
            where[AXES[1]] = 1 - here[1] if r == "pair" else here[1] - r
        if c:
            where[AXES[2]] = here[2] - c
        return where

    if n_sum > 1:
        for message in messages:
            if sum(map(bool, message)) < 2:
                continue
            both = functools.reduce(lambda p, q: p & q, exists(message, -1), True)

            def greet():
                pl.semaphore_signal(
                    barrier, inc=1, device_id=target(message), device_id_type=MESH
                )

            if both is True:
                greet()
                partners += 1
            else:
                pl.when(both)(greet)
                partners = partners + both.astype(jnp.int32)

    inputs = [
        (rocks_h, rocks),
        (table_h, table),
        (mean_h, mean0),
        (perm_h, perm),
        (wcell_h, wcell),
        (wrate_h, wrate),
        (slopes_h, slopes),
    ]
    loads = [
        pltpu.make_async_copy(a, b, in_sem.at[i]) for i, (a, b) in enumerate(inputs)
    ]
    for copy in loads:
        copy.start()

    place = [lax.broadcasted_iota(jnp.int32, tile, d) for d in range(3)]
    first_edge = [place[d] == 0 for d in range(3)]
    last_edge = [place[d] == tile[d] - 1 for d in range(3)]

    def packed(m):
        dim, _, fields = ORDER[m]
        return is_packed(dim, fields, tile)

    def copy_of(m):
        dim, direction, _ = ORDER[m]
        return pltpu.make_async_remote_copy(
            src_ref=sends[m],
            dst_ref=recvs[m],
            send_sem=send_sem.at[m],
            recv_sem=recv_sem.at[m],
            device_id={AXES[dim]: here[dim] + direction},
            device_id_type=MESH,
        )

    def reaches(a, step):
        return here[a] < counts[a] - 1 if step == 1 else here[a] > 0

    def sends_to(m):
        return reaches(*ORDER[m][:2])

    def hears_from(m):
        return reaches(ORDER[m][0], -ORDER[m][1])

    def launch(key, fields):
        m = NAMES[key]
        dim, direction, _ = ORDER[m]
        whole = fields
        kept = []
        planes = [(i, x) for i in range(len(fields)) for x in range(tx)]
        if packed(m):
            lane = place[2][0]
            pack = jnp.zeros((ty, tz), jnp.float32)
            for n, (i, x) in enumerate(planes):
                turn = n + 1 if direction == 1 else n
                part = fields[i][x]
                part = pltpu.roll(part, turn, 1) if turn else part
                pack = jnp.where(lane == n, part, pack)
            sends[m][0, 0] = pack
            fields = ()
            kept = None
        for i, field in enumerate(fields):
            if dim == 0:
                sends[m][i] = field[tx - 1 : tx] if direction == 1 else field[0:1]
                kept.append(field)
            else:
                turned = pltpu.roll(field, 1 if direction == 1 else tile[dim] - 1, dim)
                sends[m][i] = turned
                kept.append(turned)

        @pl.when(sends_to(m))
        def _():
            copy_of(m).start()

        if kept is None:
            turn = 1 if direction == 1 else tz - 1
            kept = [pltpu.roll(f, turn, 2) for f in whole]
        return kept

    def launch_all(key, fields):
        kept = [None] * 3
        for d in ROUTE:
            kept[d] = launch(key(d), fields(d))
        return kept

    def land_all(key, kept):
        got = [None] * 3
        for d in ARRIVAL:
            got[d] = land(key(d), kept[d])
        return got

    def land(key, kept):
        m = NAMES[key]
        dim, direction, _ = ORDER[m]

        @pl.when(hears_from(m))
        def _():
            copy_of(m).wait_recv()

        @pl.when(jnp.logical_not(hears_from(m)))
        def _():
            recvs[m][...] = jnp.zeros(recvs[m].shape, jnp.float32)

        out = []
        if packed(m):
            pack = recvs[m][0, 0]
        for i, field in enumerate(kept):
            if packed(m):
                parts = []
                for x in range(tx):
                    n = i * tx + x
                    turn = (tz - n) % tz if direction == 1 else tz - 1 - n
                    parts.append(pltpu.roll(pack, turn, 1) if turn else pack)
                got = jnp.stack(parts)
            else:
                got = recvs[m][i]
            if dim == 0:
                if direction == 1:
                    parts = [got, field[: tx - 1]] if tx > 1 else [got]
                else:
                    parts = [field[1:], got] if tx > 1 else [got]
                out.append(jnp.concatenate(parts, 0))
            else:
                edge = first_edge[dim] if direction == 1 else last_edge[dim]
                out.append(jnp.where(edge, got, field))
        return out

    def launch_state(s, st):
        kept = {}
        for d in (2, 0, 1):
            kept["up", d] = launch(("up", s, d), trace(st, d, 1.0))
            kept["down", d] = launch(("down", s, d), trace(st, d, -1.0))
        return kept

    def halo_copy(message):
        n = messages.index(message)
        part = parts_of[message]
        if part[0] == "whole":
            source = own_conduct.at[pl.ds(part[1], part[2])]
        else:
            source = own_parts[part]
        return pltpu.make_async_remote_copy(
            src_ref=source,
            dst_ref=halos[message],
            send_sem=halo_send.at[n],
            recv_sem=halo_recv.at[n],
            device_id=target(message),
            device_id_type=MESH,
        )

    def each_halo(sign, act, missing=None):
        groups = {}
        for message in messages:
            m, r, c = message
            apart = r if r != "pair" or len(exists(message, 1)) > bool(m) + bool(c) else 0
            groups.setdefault((m, apart, c), []).append(message)
        for group in groups.values():
            conds = exists(group[0], sign)

            def run(act=act, group=group):
                for message in group:
                    act(message)

            if not conds:
                run()
                continue
            cond = functools.reduce(lambda p, q: p & q, conds)
            pl.when(cond)(run)
            if missing is not None:
                pl.when(jnp.logical_not(cond))(functools.partial(run, missing))

    for copy in loads[:4]:
        copy.wait()
    ids = rocks[...]
    water = jnp.zeros(tile, jnp.float32)
    oil = jnp.zeros(tile, jnp.float32)
    for k in range(table.shape[1]):
        water = jnp.where(ids == k, table[0, k], water)
        oil = jnp.where(ids == k, table[1, k], oil)
    mean_sat = mean0[...]
    clipped = jnp.clip(mean_sat, 0.0, 1.0)
    mobility = water * clipped * clipped + oil * (1.0 - clipped) * (1.0 - clipped)
    conduct = [2.0 * perm[d] * mobility for d in range(3)]
    per = tz // SLOT
    row2 = place[1][0]
    lane2 = place[2][0]
    second = jnp.zeros_like(row2) + here[1] == 1
    upper_rows = row2 < ty // 2
    slot_of = lane2 // SLOT
    packs = [jnp.zeros((ty, tz), jnp.float32) for _ in range(pack_count(tile))]
    for x in range(tx):
        for f in range(3):
            own_conduct[x, f] = conduct[f][x]
            p, n = divmod(x * 3 + f, per)
            part = pltpu.roll(conduct[f][x], n * SLOT + SLOT // 2, 1)
            packs[p] = jnp.where(slot_of == n, part, packs[p])
    for part in made:
        out = own_parts[part]
        if part[0] == "half":
            tiles = [
                conduct[f][x] for x in range(part[1], part[1] + part[2]) for f in range(3)
            ]
            for j in range(0, len(tiles), 2):
                a, b = tiles[j], tiles[min(j + 1, len(tiles) - 1)]
                out[j // 2] = jnp.where(
                    upper_rows,
                    jnp.where(second, a, pltpu.roll(a, ty // 2, 0)),
                    jnp.where(second, pltpu.roll(b, ty // 2, 0), b),
                )
            continue
        for p, pack in enumerate(packs):
            top, bottom = pack[: ty // 2], pack[ty // 2 :]
            if part[0] == "strips":
                out[p] = pack
            elif part[0] == "half strips":
                out[p] = jnp.where(second[: ty // 2], top, bottom)
            else:
                turned = pltpu.roll(bottom, tz // 2, 1)
                out[p] = jnp.where(lane2[: ty // 2] < tz // 2, top, turned)

    pl.semaphore_wait(barrier, partners)
    each_halo(-1, lambda message: halo_copy(message).start())

    for copy in loads[4:]:
        copy.wait()
    state = [mean_sat] + [slopes[i] for i in range(slopes.shape[0])]

    lo, hi = -HALO, tx + HALO
    ring = (hi - lo, 2 * ty, 2 * tz)

    def position(index, size):
        return jnp.where(index < size + size // 2, index, index - 2 * size)

    n_wells = wcell.shape[1]
    nz = tz * counts[2]
    cells = wcell[...]
    line = ((cells.astype(jnp.float32) + 0.5) * (1.0 / nz)).astype(jnp.int32)
    column = cells - line * nz
    half_rates = 0.5 * wrate[...].astype(jnp.float32)
    plane_at = lax.broadcasted_iota(jnp.int32, ring[:2] + (n_wells,), 0)
    row_at = lax.broadcasted_iota(jnp.int32, ring[:2] + (n_wells,), 1)
    line_at = (here[0] * tx + lo + plane_at) * (ty * counts[1]) + (
        here[1] * ty + position(row_at, ty)
    )
    column_at = here[2] * tz + position(
        lax.broadcasted_iota(jnp.int32, (2 * tz, n_wells), 0), tz
    )
    by_line = jnp.where(line_at == line[None], half_rates[None], 0.0)
    by_line = by_line.reshape(ring[0] * ring[1], n_wells).astype(jnp.bfloat16)
    by_column = jnp.where(column_at == column, 1.0, 0.0).astype(jnp.bfloat16)
    sources = lax.dot_general(
        by_line,
        by_column,
        (((1,), (1,)), ((), ())),
        preferred_element_type=jnp.float32,
    ).reshape(ring)

    def clear(message):
        halos[message][...] = jnp.zeros(halos[message].shape, jnp.float32)

    each_halo(1, lambda message: halo_copy(message).wait_recv(), clear)

    blank = jnp.zeros((ty, tz), jnp.float32)
    from_next = lax.rem(lane2, SLOT) >= SLOT // 2
    pair_rows = jnp.where(here[1] == 0, row2, ty - 1 - row2) < ty // 2

    def rows_beyond(get):
        if counts[1] == 1:
            return blank
        if counts[1] == 2:
            return jnp.where(pair_rows, get("pair"), 0.0)
        return jnp.where(upper_rows, get(1), get(-1))

    def whole_tile(m, r, x, f):
        if (m, r) == (0, 0):
            return conduct[f][x]
        if (m, r, 0) not in halos:
            return blank
        kind, first, _ = parts_of[m, r, 0]
        if kind == "whole":
            return halos[m, r, 0][x - first, f]
        j, h = divmod(3 * (x - first) + f, 2)
        folded = halos[m, r, 0][j]
        turned = pltpu.roll(folded, ty // 2, 0)
        return jnp.where(second, *((folded, turned) if h else (turned, folded)))

    def pack_tile(m, r, p):
        sides = []
        for c in (1, -1):
            if (m, r, c) not in halos:
                sides.append(blank)
                continue
            got = halos[m, r, c][p]
            kind = parts_of[m, r, c][0]
            if kind == "half strips":
                got = jnp.concatenate([got, got], 0)
            elif kind == "folded strips":
                got = jnp.concatenate([got, pltpu.roll(got, tz // 2, 1)], 0)
            sides.append(got)
        return jnp.where(from_next, *sides)

    merged = {}

    def side_tile(m, beyond, x, f):
        p, n = divmod(x * 3 + f, per)
        if (m, beyond, p) not in merged:
            get = functools.partial(lambda r: pack_tile(m, r, p))
            merged[m, beyond, p] = rows_beyond(get) if beyond else get(0)
        tile2 = merged[m, beyond, p]
        return pltpu.roll(tile2, tz - n * SLOT - SLOT // 2, 1)

    def ring_plane(p, f):
        m, x = divmod(p, tx)
        near = [whole_tile(m, 0, x, f), side_tile(m, False, x, f)]
        far = [rows_beyond(lambda r: whole_tile(m, r, x, f)), side_tile(m, True, x, f)]
        return jnp.concatenate(
            [jnp.concatenate(near, 1), jnp.concatenate(far, 1)], 0
        )

    cond = [
        Slab(lo, jnp.stack([ring_plane(p, f) for p in range(lo, hi)])) for f in range(3)
    ]
    full = 2.0 * (cond[0].data + cond[1].data + cond[2].data)
    inv_total = Slab(lo, jnp.where(full > 0.0, invert(full), 0.0))
    weighted = Slab(lo, sources * inv_total.data)
    third = Slab(lo, inv_total.data * (1.0 / 3.0))
    half_inv = [
        Slab(lo, jnp.where(c.data > 0.0, 0.5 * invert(c.data), 0.0)) for c in cond
    ]

    def own(data, at=0):
        return data[at : at + tx, :ty, :tz]

    def own_of(slab):
        return own(slab.data, -slab.lo)

    def precondition(r, lo, hi):
        shared = (r[0] + r[1] + r[2]) * third.get(lo, hi)
        return [Slab(lo, r[d] * half_inv[d].get(lo, hi) + shared) for d in range(3)]

    hi -= 1
    load = []
    for d in range(3):
        lift = weighted.data + GRAVITY[d] if GRAVITY[d] else weighted.data
        drop = weighted.data - GRAVITY[d] if GRAVITY[d] else weighted.data
        after = following_of(d, Slab(-HALO, cond[d].data * lift), lo, hi)
        load.append(cond[d].get(lo, hi) * drop[: hi - lo] + after)
    vector = precondition(load, lo, hi)
    load = [own(r, -lo) for r in load]
    both = [
        Slab(lo + 1, cond[d].get(lo + 1, hi - 1) + following_of(d, cond[d], lo + 1, hi - 1))
        for d in range(3)
    ]
    basis, images, priors, means = [], [], [], []
    for k in range(ITERS):
        lo += 1
        previous = [previous_of(d, vector[d], lo, hi) for d in range(3)]
        total = sum(
            cond[d].get(lo, hi) * (vector[d].get(lo, hi) + previous[d]) for d in range(3)
        )
        mean = Slab(lo, total * inv_total.get(lo, hi))
        basis.append([own_of(v) for v in vector])
        priors.append([own(p, -lo) for p in previous])
        means.append(mean)
        if k + 1 == ITERS:
            break
        hi -= 1
        image = []
        for d in range(3):
            spread = Slab(lo, cond[d].get(lo, hi + 1) * mean.data)
            image.append(
                both[d].get(lo, hi) * vector[d].get(lo, hi)
                - (spread.get(lo, hi) + following_of(d, spread, lo, hi))
            )
        images.append([own(g, -lo) for g in image])
        fresh = precondition(image, lo, hi)
        vector = [
            Slab(lo, fresh[d].data - SHIFT * vector[d].get(lo, hi)) for d in range(3)
        ]
    center = own_of(means[-1])

    def dot(a, b):
        both = jnp.sum(a[0] * b[0] + a[1] * b[1] + a[2] * b[2], axis=0)
        return jnp.sum(both, axis=0, keepdims=True)

    def place_in(dims):
        slot = 0
        for d in dims:
            slot = slot * counts[d] + here[d]
        return slot

    def send_sum(p, step):
        slot = place_in(phases[p])
        return pltpu.make_async_remote_copy(
            src_ref=sums[p].at[slot],
            dst_ref=sums[p].at[slot],
            send_sem=sum_send.at[p],
            recv_sem=sum_recv.at[p],
            device_id=peer_of(step),
            device_id_type=MESH,
        )

    def all_sums(p, sem):
        others_of = sums[p].at[pl.ds(0, sums[p].shape[0] - 1)]
        return pltpu.make_async_copy(others_of, others_of, sem.at[p])

    at_start = [here[d] * tile[d] + place[d] == 0 for d in range(3)]

    def flux_parts(d, m, m_next, m_back, v, v_back):
        after = conduct[d] * (m - v) + beyond[d] * (v - m_next)
        prior = prior_c[d] * (m_back - v_back) + conduct[d] * (v_back - m)
        return 0.5 * after, jnp.where(at_start[d], 0.0, 0.5 * prior)

    def neighbours(slab):
        after = [own(following_of(d, slab, 0, tx)) for d in range(3)]
        prior = [own(previous_of(d, slab, 0, tx)) for d in range(3)]
        return after, prior

    beyond = [own(following_of(d, cond[d], 0, tx)) for d in range(3)]
    prior_c = [own(previous_of(d, cond[d], 0, tx)) for d in range(3)]

    def prepare():
        state_kept = launch_state(0, state)
        ahead = launch_all(lambda d: ("mean", d), lambda d: [center])
        behind = launch_all(lambda d: ("back", d), lambda d: [center])
        cube = cube_moments(state, water, oil)
        faces = stage_faces(0, state, state_kept)
        moments = cube, [[square_moments(f, water, oil) for f in four] for four in faces]
        each_halo(-1, lambda message: halo_copy(message).wait_send())
        parts = [[None] * (ITERS + 1) for _ in range(3)]
        w_next, w_back = neighbours(weighted)
        w = own_of(weighted)
        for d in range(3):
            g = GRAVITY[d]
            after = conduct[d] * (w - g) - beyond[d] * (w_next[d] + g)
            prior = prior_c[d] * (w_back[d] - g) - conduct[d] * (w + g)
            parts[d][ITERS] = 0.5 * after, jnp.where(at_start[d], 0.0, 0.5 * prior)
        for k in range(ITERS):
            if k + 1 < ITERS:
                m_next, m_back = neighbours(means[k])
            else:
                m_next = [got[0] for got in land_all(lambda d: ("mean", d), ahead)]
                m_back = [got[0] for got in land_all(lambda d: ("back", d), behind)]
            m = own_of(means[k])
            for d in range(3):
                parts[d][k] = flux_parts(
                    d, m, m_next[d], m_back[d], basis[k][d], priors[k][d]
                )
        return parts, moments

    def stage_faces(s, st, kept):
        faces = [None] * 3
        for d in (1, 0, 2):
            faces[d] = (
                trace(st, d, 1.0),
                land(("down", s, d), kept["down", d]),
                land(("up", s, d), kept["up", d]),
                trace(st, d, -1.0),
            )
        return faces

    source = own(sources, HALO)

    pairs = [(i, j) for i in range(ITERS) for j in range(i, ITERS)]
    rows = [dot(basis[j], images[i]) for i, j in pairs[:-1]]
    gaps = [part - center for part in basis[-1] + priors[-1]]
    rows.append(dot([conduct[d] * gaps[d] for d in range(3)], gaps[:3]))
    rows[-1] = rows[-1] + dot([conduct[d] * gaps[3 + d] for d in range(3)], gaps[3:])
    rows += [dot(basis[i], load) for i in range(ITERS)]
    acc = jnp.concatenate(rows + [jnp.zeros_like(rows[0])] * (-len(rows) % 8), 0)
    diag = lax.broadcasted_iota(jnp.int32, acc.shape, 0) == lax.broadcasted_iota(
        jnp.int32, acc.shape, 1
    )
    spread = acc.shape
    acc = jnp.where(diag, jnp.sum(acc, axis=1, keepdims=True), 0.0)
    acc = jnp.sum(acc, axis=0, keepdims=True)
    early = None
    for p, dims in enumerate(phases):
        sums[p][place_in(dims)] = acc
        for step in sorted(peers(dims, counts), key=farness):
            send_sum(p, step).start()
        if early is None:
            early = prepare()
        all_sums(p, sum_recv).wait()
        parts = [sums[p][j] for j in range(sums[p].shape[0])]
        while len(parts) > 1:
            parts = [sum(parts[j : j + 2]) for j in range(0, len(parts), 2)]
        acc = parts[0]
    early = early or prepare()
    parts, moments = early
    full = jnp.where(diag, jnp.broadcast_to(acc, spread), 0.0)
    full = jnp.broadcast_to(jnp.sum(full, axis=1, keepdims=True), spread)
    gram = {}
    for r, (i, j) in enumerate(pairs):
        gram[i, j] = full[r : r + 1]
    right = [full[len(pairs) + i : len(pairs) + i + 1] for i in range(ITERS)]

    factor, pivot = {}, {}
    for i in range(ITERS):
        pivot[i] = invert(gram[i, i])
        for j in range(i + 1, ITERS):
            factor[j, i] = gram[i, j] * pivot[i]
        for j in range(i + 1, ITERS):
            for m in range(j, ITERS):
                gram[j, m] = gram[j, m] - factor[j, i] * gram[i, m]
            right[j] = right[j] - factor[j, i] * right[i]
    coef = [None] * ITERS
    for i in reversed(range(ITERS)):
        value = right[i] * pivot[i]
        for j in range(i + 1, ITERS):
            value = value - factor[j, i] * coef[j]
        coef[i] = value
    coef = [jnp.broadcast_to(c, (ty, tz))[None] for c in coef]

    def combine(parts):
        out = coef[0] * parts[0]
        for j in range(1, ITERS):
            out = out + coef[j] * parts[j]
        return out

    fluxes, before = [None] * 3, [None] * 3
    for d in range(3):
        traces_o[d] = combine([p[d] for p in basis])
        fluxes[d] = combine([p[0] for p in parts[d][:ITERS]]) + parts[d][ITERS][0]
        before[d] = combine([p[1] for p in parts[d][:ITERS]]) + parts[d][ITERS][1]
        flux_o[d] = fluxes[d]
    after_pos = [fluxes[d] > 0.0 for d in range(3)]
    before_pos = [before[d] > 0.0 for d in range(3)]
    mid_speed = [0.5 * (before[d] + fluxes[d]) for d in range(3)]
    dif_speed = [0.5 * (fluxes[d] - before[d]) for d in range(3)]

    def rate(s, st, kept=None, moments=None):
        if moments is None:
            cube = cube_moments(st, water, oil)
            faces = stage_faces(s, st, kept)
        else:
            cube, squares = moments
        m1, mlin, msqr, mmix = cube
        out = [jnp.where(source > 0.0, source, source * frac(st[0], water, oil))] + [None] * 9
        for d in range(3):
            out[LIN[d]] = 2.0 * (mid_speed[d] * m1 + dif_speed[d] * mlin[d])
            out[SQR[d]] = 6.0 * (mid_speed[d] * mlin[d] + dif_speed[d] * msqr[d])
        for a, b in MIX:
            m = mmix[a, b]
            out[MIX[a, b]] = 2.0 * (
                mid_speed[a] * mlin[b]
                + dif_speed[a] * m
                + mid_speed[b] * mlin[a]
                + dif_speed[b] * m
            )
        for d in (1, 0, 2):
            e, f = others(d)
            pick = lambda flag, a, b: [jnp.where(flag, p, q) for p, q in zip(a, b)]
            if moments is None:
                upper, after, prior, lower = faces[d]
                o = square_moments(pick(after_pos[d], upper, after), water, oil)
                i = square_moments(pick(before_pos[d], prior, lower), water, oil)
            else:
                upper, after, prior, lower = squares[d]
                o = pick(after_pos[d], upper, after)
                i = pick(before_pos[d], prior, lower)
            o = [fluxes[d] * m for m in o]
            i = [before[d] * m for m in i]
            out[0] = out[0] + (i[0] - o[0])
            out[SQR[d]] = out[SQR[d]] + (i[0] - o[0])
            out[LIN[d]] = out[LIN[d]] - (i[0] + o[0])
            out[LIN[e]] = out[LIN[e]] + (i[1] - o[1])
            out[LIN[f]] = out[LIN[f]] + (i[2] - o[2])
            out[mix(d, e)] = out[mix(d, e)] - (i[1] + o[1])
            out[mix(d, f)] = out[mix(d, f)] - (i[2] + o[2])
            out[SQR[e]] = out[SQR[e]] + (i[3] - o[3])
            out[SQR[f]] = out[SQR[f]] + (i[4] - o[4])
            out[mix(e, f)] = out[mix(e, f)] + (i[5] - o[5])
        return [(STEP * MASS[m]) * out[m] for m in range(10)]

    def drain(*kinds):
        for key, m in NAMES.items():
            if key[0] in kinds or len(key) == 3 and key[1] in kinds:

                @pl.when(sends_to(m))
                def _():
                    copy_of(m).wait_send()

    change = rate(0, state, moments=moments)
    first = [state[m] + change[m] for m in range(10)]
    kept = launch_state(1, first)
    drain("mean", "back", 0)
    change = rate(1, first, kept)
    second = [0.75 * state[m] + 0.25 * (first[m] + change[m]) for m in range(10)]
    kept = launch_state(2, second)
    drain(1)
    for p in range(n_sum):
        all_sums(p, sum_send).wait()
    change = rate(2, second, kept)
    for m in range(10):
        sat_o[m] = (1.0 / 3.0) * state[m] + (2.0 / 3.0) * (second[m] + change[m])

    drain(2)


def hand_on(a, b, c, a_out, b_out, c_out):
    a_out[...] = a[...]
    b_out[...] = b[...]
    c_out[...] = c[...]


def per_device(counts, perm, mean0, slopes, rocks, table, wcell, wrate):
    tile = mean0.shape
    f32 = jnp.float32
    bufs = [
        pltpu.VMEM(buffer_shape(dim, f, tile), f32) for dim, _, f in ORDER
    ]
    phases = sum_phases(counts)
    sums = [pltpu.VMEM((len(peers(p, counts)) + 1, 1, tile[2]), f32) for p in phases]
    messages = halo_messages(counts, tile[0])
    parts = [halo_part(m, tile) for m in messages]
    halos = [pltpu.VMEM(part_shape(p, tile), f32) for p in parts]
    made = sorted({p for p in parts if p[0] != "whole"})
    own_halo = [pltpu.VMEM((tile[0], 3) + tile[1:], f32)]
    own_halo += [pltpu.VMEM(part_shape(p, tile), f32) for p in made]
    wcell, wrate = wcell.reshape(1, -1), wrate.reshape(1, -1)
    operands = (perm, mean0, slopes, rocks, table, wcell, wrate)
    copies = [
        (pltpu.SMEM if a is table else pltpu.VMEM)(a.shape, a.dtype) for a in operands
    ]
    vmem = pl.BlockSpec(memory_space=pltpu.VMEM)
    hbm = pl.BlockSpec(memory_space=pltpu.HBM)
    dma = pltpu.SemaphoreType.DMA
    shapes = tuple(jax.ShapeDtypeStruct((n,) + tile, f32) for n in (3, 3, 10))
    results = pl.pallas_call(
        functools.partial(kernel, counts, messages),
        out_shape=tuple(pltpu.VMEM(s.shape, f32) for s in shapes),
        in_specs=[hbm] * len(operands),
        out_specs=(vmem,) * 3,
        scratch_shapes=bufs
        + bufs
        + sums
        + halos
        + own_halo
        + copies
        + [dma((len(ORDER),))] * 2
        + [dma((max(1, len(phases)),))] * 2
        + [dma((len(messages),))] * 2
        + [dma((len(operands),))],
        compiler_params=pltpu.CompilerParams(collective_id=0, has_side_effects=True),
    )(*operands)
    results = [pltpu.with_memory_space_constraint(r, pltpu.VMEM) for r in results]
    return pl.pallas_call(
        hand_on, out_shape=shapes, in_specs=[vmem] * 3, out_specs=(vmem,) * 3
    )(*results)


def solution(mesh):
    counts = tuple(mesh.shape[a] for a in AXES)
    grid = P(None, "gx", "gy", "gz")
    cells = P("gx", "gy", "gz")
    return jax.shard_map(
        functools.partial(per_device, counts),
        mesh=mesh,
        in_specs=(grid, cells, grid, cells, P(), P(), P()),
        out_specs=(grid, grid, grid),
        check_vma=False,
    )
```

```python
import functools
import itertools

import jax
import jax.numpy as jnp
import numpy as np
from jax import lax
from jax.experimental import pallas as pl
from jax.experimental.pallas import tpu as pltpu
from jax.sharding import PartitionSpec as P

ITERS = 3
STEP = 0.05
GRAVITY = (0.0, 0.0, 2.0)
SHIFT = 0.6
ROUTE = (2, 0, 1)
ARRIVAL = (1, 0, 2)
AXES = ("gx", "gy", "gz")
MESH = pl.DeviceIdType.MESH
ROOT = float(np.sqrt(0.6))
XI = (-ROOT, 0.0, ROOT)
LEG2 = (0.4, -0.5, 0.4)
WEIGHT = (5.0 / 18.0, 8.0 / 18.0, 5.0 / 18.0)

LIN = (1, 2, 3)
SQR = (4, 5, 6)
MIX = {(0, 1): 7, (0, 2): 8, (1, 2): 9}
MASS = (1.0, 3.0, 3.0, 3.0, 5.0, 5.0, 5.0, 9.0, 9.0, 9.0)


def mix(a, b):
    return MIX[(min(a, b), max(a, b))]


def others(d):
    return [e for e in range(3) if e != d]


HALO = ITERS
SLOT = 8


def message_list():
    names = {}
    order = []

    def add(key, dim, direction, fields):
        names[key] = len(order)
        order.append((dim, direction, fields))

    for d in range(3):
        add(("mean", d), d, -1, 1)
        add(("back", d), d, 1, 1)
    for s in range(3):
        for d in range(3):
            add(("up", s, d), d, 1, 6)
            add(("down", s, d), d, -1, 6)
    return names, order


NAMES, ORDER = message_list()
DIRECT = 64


def sum_phases(counts):
    split = [d for d in range(3) if counts[d] > 1]
    if int(np.prod(counts)) <= DIRECT:
        return [tuple(split)] if split else []
    return [(d,) for d in (1, 2, 0) if counts[d] > 1]


def peers(dims, counts):
    steps = itertools.product(*[range(counts[d]) for d in dims])
    return [dict(zip(dims, s)) for s in steps if any(s)]


def layers(m, tx):
    return tx if m == 0 else max(0, min(tx, HALO - (abs(m) - 1) * tx))


def halo_messages(counts, tx):
    reach = min(-(-HALO // tx), counts[0] - 1)
    rows = {1: (0,), 2: (0, "pair")}.get(counts[1], (0, 1, -1))
    columns = (0, 1, -1) if counts[2] > 1 else (0,)
    found = []
    for m in sorted(range(-reach, reach + 1), key=lambda m: -abs(m)):
        full = m != 0 and (abs(m) - 1) * tx + 1 >= HALO
        side = 1 if m > 0 else -1
        for c in columns:
            for r in rows:
                spare = full and side in (c, r)
                if not spare and (m, r, c) != (0, 0, 0):
                    found.append((m, r, c))
    return sorted(found, key=lambda t: (t[2] == 0, t[0] > 0, -abs(t[0])))


def pack_count(tile):
    return -(-3 * tile[0] // (tile[2] // SLOT))


def halo_part(message, tile):
    m, r, c = message
    count = layers(m, tile[0])
    first = tile[0] - count if m < 0 else 0
    if c == 0:
        return ("half" if r == "pair" else "whole", first, count)
    if r == "pair":
        return ("half strips",)
    folds = r == 0 and 6 * tile[0] * SLOT <= tile[2]
    return ("folded strips",) if folds else ("strips",)


def part_shape(part, tile):
    tx, ty, tz = tile
    if part[0] == "whole":
        return (part[2], 3, ty, tz)
    if part[0] == "half":
        return ((3 * part[2] + 1) // 2, ty, tz)
    return (pack_count(tile), ty if part[0] == "strips" else ty // 2, tz)


class Slab:
    def __init__(self, lo, data):
        self.lo = lo
        self.data = data

    def get(self, lo, hi):
        return self.data[lo - self.lo : hi - self.lo]


def following_of(d, slab, lo, hi):
    if d == 0:
        return slab.get(lo + 1, hi + 1)
    part = slab.get(lo, hi)
    return pltpu.roll(part, part.shape[d] - 1, d)


def previous_of(d, slab, lo, hi):
    if d == 0:
        return slab.get(lo - 1, hi - 1)
    return pltpu.roll(slab.get(lo, hi), 1, d)


def invert(x):
    return pl.reciprocal(x, approx=True)


def frac(sat, ratio):
    c = jnp.clip(sat, 0.0, 1.0)
    w = c * c
    r = 1.0 - c
    return w * invert(w + ratio * r * r)


def trace(state, d, sign):
    e, f = others(d)
    return [
        (state[0] + state[SQR[d]]) + sign * state[LIN[d]],
        state[LIN[e]] + sign * state[mix(d, e)],
        state[LIN[f]] + sign * state[mix(d, f)],
        state[SQR[e]],
        state[SQR[f]],
        state[mix(e, f)],
    ]


def square_moments(coefs, ratio):
    base, s, t, ss, tt, st = coefs
    firsts, seconds, thirds = [], [], []
    for i in range(3):
        if i == 1:
            a = base + LEG2[1] * ss
            b = t
        else:
            a = base + XI[i] * s + LEG2[i] * ss
            b = t + XI[i] * st
        outer = a + LEG2[0] * tt
        lean = ROOT * b
        low = frac(outer - lean, ratio)
        mid = frac(a + LEG2[1] * tt, ratio)
        high = frac(outer + lean, ratio)
        both = low + high
        firsts.append(WEIGHT[0] * both + WEIGHT[1] * mid)
        seconds.append((WEIGHT[0] * ROOT) * (high - low))
        thirds.append((WEIGHT[0] * LEG2[0]) * both + (WEIGHT[1] * LEG2[1]) * mid)
    ends = firsts[0] + firsts[2]
    m00 = WEIGHT[0] * ends + WEIGHT[1] * firsts[1]
    m10 = (WEIGHT[0] * ROOT) * (firsts[2] - firsts[0])
    m20 = (WEIGHT[0] * LEG2[0]) * ends + (WEIGHT[1] * LEG2[1]) * firsts[1]
    m01 = WEIGHT[0] * (seconds[0] + seconds[2]) + WEIGHT[1] * seconds[1]
    m11 = (WEIGHT[0] * ROOT) * (seconds[2] - seconds[0])
    m02 = WEIGHT[0] * (thirds[0] + thirds[2]) + WEIGHT[1] * thirds[1]
    return m00, m10, m01, m20, m02, m11


def cube_moments(state, ratio):
    c0, cx, cy, cz, cxx, cyy, czz, cxy, cxz, cyz = state
    w, v, q = WEIGHT[0], WEIGHT[1], WEIGHT[0] * 0.6
    planes = []
    for i in range(3):
        if i == 1:
            a = c0 + LEG2[1] * cxx
            by, bz = cy, cz
        else:
            a = c0 + XI[i] * cx + LEG2[i] * cxx
            by = cy + XI[i] * cxy
            bz = cz + XI[i] * cxz
        rows = []
        for j in range(3):
            if j == 1:
                b = a + LEG2[1] * cyy
                g = bz
            else:
                b = a + XI[j] * by + LEG2[j] * cyy
                g = bz + XI[j] * cyz
            edge = b + LEG2[0] * czz
            lean = ROOT * g
            low = frac(edge - lean, ratio)
            mid = frac(b + LEG2[1] * czz, ratio)
            high = frac(edge + lean, ratio)
            both = low + high
            rows.append((w * both + v * mid, (w * ROOT) * (high - low), q * both))
        r0, r1, r2 = zip(*rows)
        planes.append(
            (
                w * (r0[0] + r0[2]) + v * r0[1],
                (w * ROOT) * (r0[2] - r0[0]),
                q * (r0[0] + r0[2]),
                w * (r1[0] + r1[2]) + v * r1[1],
                (w * ROOT) * (r1[2] - r1[0]),
                w * (r2[0] + r2[2]) + v * r2[1],
            )
        )
    p00, p10, p20, p01, p11, p02 = zip(*planes)

    def even(p):
        return w * (p[0] + p[2]) + v * p[1]

    def odd(p):
        return (w * ROOT) * (p[2] - p[0])

    m1 = even(p00)
    mlin = (odd(p00), even(p10), even(p01))
    msqr = (q * (p00[0] + p00[2]), even(p20), even(p02))
    mmix = {(0, 1): odd(p10), (0, 2): odd(p01), (1, 2): even(p11)}
    return m1, mlin, msqr, mmix


def is_packed(dim, fields, tile):
    return dim == 2 and fields > 2 and fields * tile[0] < tile[2]


def buffer_shape(dim, fields, tile):
    if is_packed(dim, fields, tile):
        return (1, 1, tile[1], tile[2])
    return (fields, 1 if dim == 0 else tile[0], tile[1], tile[2])


def kernel(counts, messages, perm_h, mean_h, slopes_h, rocks_h, table_h, wcell_h, wrate_h, *rest):
    n_msg = len(ORDER)
    rest = list(rest)

    def take(n):
        part = rest[:n]
        del rest[:n]
        return part

    traces_o, flux_o, sat_o = take(3)
    sends, recvs = take(n_msg), take(n_msg)
    phases = sum_phases(counts)
    n_sum = len(phases)
    sums = take(n_sum)
    halos = dict(zip(messages, take(len(messages))))
    parts_of = {message: halo_part(message, mean_h.shape) for message in messages}
    made = sorted({p for p in parts_of.values() if p[0] != "whole"})
    own_conduct = take(1)[0]
    own_parts = dict(zip(made, take(len(made))))
    perm, mean0, slopes, rocks, table, wcell, wrate = take(7)
    send_sem, recv_sem, sum_send, sum_recv, halo_send, halo_recv, in_sem = rest
    tile = mean0.shape
    tx, ty, tz = tile
    here = [lax.axis_index(a) for a in AXES]

    barrier = pltpu.get_barrier_semaphore()
    partners = 0

    def nearness(step):
        return sum(min(s, counts[d] - s) for d, s in step.items())

    def farness(step):
        return -sum(counts[d] - s for d, s in step.items() if s)

    def peer_of(step):
        return {AXES[d]: lax.rem(here[d] + s, counts[d]) for d, s in step.items()}

    for dims in phases:
        for step in sorted(peers(dims, counts), key=nearness):
            pl.semaphore_signal(
                barrier, inc=1, device_id=peer_of(step), device_id_type=MESH
            )
            partners += 1

    def inside(a, step):
        if step == 0:
            return []
        return [here[a] + step >= 0 if step < 0 else here[a] + step < counts[a]]

    def exists(message, sign):
        m, r, c = message
        found = inside(0, sign * m) + inside(2, sign * c)
        if r != "pair":
            return found + inside(1, sign * r)
        if m and (abs(m) - 1) * mean_h.shape[0] + 1 >= HALO:
            found.append(here[1] == int((m > 0) == (sign > 0)))
        return found

    def target(message):
        m, r, c = message
        where = {}
        if m:
            where[AXES[0]] = here[0] - m
        if r:
            where[AXES[1]] = 1 - here[1] if r == "pair" else here[1] - r
        if c:
            where[AXES[2]] = here[2] - c
        return where

    if n_sum > 1:
        for message in messages:
            if sum(map(bool, message)) < 2:
                continue
            both = functools.reduce(lambda p, q: p & q, exists(message, -1), True)

            def greet():
                pl.semaphore_signal(
                    barrier, inc=1, device_id=target(message), device_id_type=MESH
                )

            if both is True:
                greet()
                partners += 1
            else:
                pl.when(both)(greet)
                partners = partners + both.astype(jnp.int32)

    inputs = [
        (rocks_h, rocks),
        (table_h, table),
        (mean_h, mean0),
        (perm_h, perm),
        (wcell_h, wcell),
        (wrate_h, wrate),
        (slopes_h, slopes),
    ]
    loads = [
        pltpu.make_async_copy(a, b, in_sem.at[i]) for i, (a, b) in enumerate(inputs)
    ]
    for copy in loads:
        copy.start()

    place = [lax.broadcasted_iota(jnp.int32, tile, d) for d in range(3)]
    first_edge = [place[d] == 0 for d in range(3)]
    last_edge = [place[d] == tile[d] - 1 for d in range(3)]

    def packed(m):
        dim, _, fields = ORDER[m]
        return is_packed(dim, fields, tile)

    def copy_of(m):
        dim, direction, _ = ORDER[m]
        return pltpu.make_async_remote_copy(
            src_ref=sends[m],
            dst_ref=recvs[m],
            send_sem=send_sem.at[m],
            recv_sem=recv_sem.at[m],
            device_id={AXES[dim]: here[dim] + direction},
            device_id_type=MESH,
        )

    def reaches(a, step):
        return here[a] < counts[a] - 1 if step == 1 else here[a] > 0

    def sends_to(m):
        return reaches(*ORDER[m][:2])

    def hears_from(m):
        return reaches(ORDER[m][0], -ORDER[m][1])

    def launch(key, fields):
        m = NAMES[key]
        dim, direction, _ = ORDER[m]
        whole = fields
        kept = []
        planes = [(i, x) for i in range(len(fields)) for x in range(tx)]
        if packed(m):
            lane = place[2][0]
            pack = jnp.zeros((ty, tz), jnp.float32)
            for n, (i, x) in enumerate(planes):
                turn = n + 1 if direction == 1 else n
                part = fields[i][x]
                part = pltpu.roll(part, turn, 1) if turn else part
                pack = jnp.where(lane == n, part, pack)
            sends[m][0, 0] = pack
            fields = ()
            kept = None
        for i, field in enumerate(fields):
            if dim == 0:
                sends[m][i] = field[tx - 1 : tx] if direction == 1 else field[0:1]
                kept.append(field)
            else:
                turned = pltpu.roll(field, 1 if direction == 1 else tile[dim] - 1, dim)
                sends[m][i] = turned
                kept.append(turned)

        @pl.when(sends_to(m))
        def _():
            copy_of(m).start()

        if kept is None:
            turn = 1 if direction == 1 else tz - 1
            kept = [pltpu.roll(f, turn, 2) for f in whole]
        return kept

    def launch_all(key, fields):
        kept = [None] * 3
        for d in ROUTE:
            kept[d] = launch(key(d), fields(d))
        return kept

    def land_all(key, kept):
        got = [None] * 3
        for d in ARRIVAL:
            got[d] = land(key(d), kept[d])
        return got

    def arrive(m):

        @pl.when(hears_from(m))
        def _():
            copy_of(m).wait_recv()

        @pl.when(jnp.logical_not(hears_from(m)))
        def _():
            recvs[m][...] = jnp.zeros(recvs[m].shape, jnp.float32)

    def land_planes(key):
        m = NAMES[key]
        arrive(m)
        return [recvs[m][i] for i in range(recvs[m].shape[0])]

    def land(key, kept):
        m = NAMES[key]
        dim, direction, _ = ORDER[m]
        arrive(m)
        out = []
        if packed(m):
            pack = recvs[m][0, 0]
        for i, field in enumerate(kept):
            if packed(m):
                parts = []
                for x in range(tx):
                    n = i * tx + x
                    turn = (tz - n) % tz if direction == 1 else tz - 1 - n
                    parts.append(pltpu.roll(pack, turn, 1) if turn else pack)
                got = jnp.stack(parts)
            else:
                got = recvs[m][i]
            if dim == 0:
                if direction == 1:
                    parts = [got, field[: tx - 1]] if tx > 1 else [got]
                else:
                    parts = [field[1:], got] if tx > 1 else [got]
                out.append(jnp.concatenate(parts, 0))
            else:
                edge = first_edge[dim] if direction == 1 else last_edge[dim]
                out.append(jnp.where(edge, got, field))
        return out

    def launch_state(s, st):
        kept = {}
        for d in (2, 0, 1):
            kept["up", d] = launch(("up", s, d), trace(st, d, 1.0))
            kept["down", d] = launch(("down", s, d), trace(st, d, -1.0))
        return kept

    def halo_copy(message):
        n = messages.index(message)
        part = parts_of[message]
        if part[0] == "whole":
            source = own_conduct.at[pl.ds(part[1], part[2])]
        else:
            source = own_parts[part]
        return pltpu.make_async_remote_copy(
            src_ref=source,
            dst_ref=halos[message],
            send_sem=halo_send.at[n],
            recv_sem=halo_recv.at[n],
            device_id=target(message),
            device_id_type=MESH,
        )

    def each_halo(sign, act, missing=None):
        groups = {}
        for message in messages:
            m, r, c = message
            apart = r if r != "pair" or len(exists(message, 1)) > bool(m) + bool(c) else 0
            groups.setdefault((m, apart, c), []).append(message)
        for group in groups.values():
            conds = exists(group[0], sign)

            def run(act=act, group=group):
                for message in group:
                    act(message)

            if not conds:
                run()
                continue
            cond = functools.reduce(lambda p, q: p & q, conds)
            pl.when(cond)(run)
            if missing is not None:
                pl.when(jnp.logical_not(cond))(functools.partial(run, missing))

    for copy in loads[:4]:
        copy.wait()
    ids = rocks[...]
    water = jnp.zeros(tile, jnp.float32)
    oil = jnp.zeros(tile, jnp.float32)
    for k in range(table.shape[1]):
        water = jnp.where(ids == k, table[0, k], water)
        oil = jnp.where(ids == k, table[1, k], oil)
    ratio = oil * invert(water)
    mean_sat = mean0[...]
    clipped = jnp.clip(mean_sat, 0.0, 1.0)
    mobility = water * clipped * clipped + oil * (1.0 - clipped) * (1.0 - clipped)
    conduct = [2.0 * perm[d] * mobility for d in range(3)]
    per = tz // SLOT
    row2 = place[1][0]
    lane2 = place[2][0]
    second = jnp.zeros_like(row2) + here[1] == 1
    upper_rows = row2 < ty // 2
    slot_of = lane2 // SLOT
    packs = [jnp.zeros((ty, tz), jnp.float32) for _ in range(pack_count(tile))]
    for x in range(tx):
        for f in range(3):
            own_conduct[x, f] = conduct[f][x]
            p, n = divmod(x * 3 + f, per)
            part = pltpu.roll(conduct[f][x], n * SLOT + SLOT // 2, 1)
            packs[p] = jnp.where(slot_of == n, part, packs[p])
    for part in made:
        out = own_parts[part]
        if part[0] == "half":
            tiles = [
                conduct[f][x] for x in range(part[1], part[1] + part[2]) for f in range(3)
            ]
            for j in range(0, len(tiles), 2):
                a, b = tiles[j], tiles[min(j + 1, len(tiles) - 1)]
                out[j // 2] = jnp.where(
                    upper_rows,
                    jnp.where(second, a, pltpu.roll(a, ty // 2, 0)),
                    jnp.where(second, pltpu.roll(b, ty // 2, 0), b),
                )
            continue
        for p, pack in enumerate(packs):
            top, bottom = pack[: ty // 2], pack[ty // 2 :]
            if part[0] == "strips":
                out[p] = pack
            elif part[0] == "half strips":
                out[p] = jnp.where(second[: ty // 2], top, bottom)
            else:
                turned = pltpu.roll(bottom, tz // 2, 1)
                out[p] = jnp.where(lane2[: ty // 2] < tz // 2, top, turned)

    pl.semaphore_wait(barrier, partners)
    each_halo(-1, lambda message: halo_copy(message).start())

    for copy in loads[4:]:
        copy.wait()
    state = [mean_sat] + [slopes[i] for i in range(slopes.shape[0])]

    lo, hi = -HALO, tx + HALO
    ring = (hi - lo, 2 * ty, 2 * tz)

    def position(index, size):
        return jnp.where(index < size + size // 2, index, index - 2 * size)

    n_wells = wcell.shape[1]
    nz = tz * counts[2]
    cells = wcell[...]
    line = ((cells.astype(jnp.float32) + 0.5) * (1.0 / nz)).astype(jnp.int32)
    column = cells - line * nz
    half_rates = 0.5 * wrate[...].astype(jnp.float32)
    plane_at = lax.broadcasted_iota(jnp.int32, ring[:2] + (n_wells,), 0)
    row_at = lax.broadcasted_iota(jnp.int32, ring[:2] + (n_wells,), 1)
    line_at = (here[0] * tx + lo + plane_at) * (ty * counts[1]) + (
        here[1] * ty + position(row_at, ty)
    )
    column_at = here[2] * tz + position(
        lax.broadcasted_iota(jnp.int32, (2 * tz, n_wells), 0), tz
    )
    by_line = jnp.where(line_at == line[None], half_rates[None], 0.0)
    by_line = by_line.reshape(ring[0] * ring[1], n_wells).astype(jnp.bfloat16)
    by_column = jnp.where(column_at == column, 1.0, 0.0).astype(jnp.bfloat16)
    sources = lax.dot_general(
        by_line,
        by_column,
        (((1,), (1,)), ((), ())),
        preferred_element_type=jnp.float32,
    ).reshape(ring)

    def clear(message):
        halos[message][...] = jnp.zeros(halos[message].shape, jnp.float32)

    each_halo(1, lambda message: halo_copy(message).wait_recv(), clear)

    blank = jnp.zeros((ty, tz), jnp.float32)
    from_next = lax.rem(lane2, SLOT) >= SLOT // 2
    pair_rows = jnp.where(here[1] == 0, row2, ty - 1 - row2) < ty // 2

    def rows_beyond(get):
        if counts[1] == 1:
            return blank
        if counts[1] == 2:
            return jnp.where(pair_rows, get("pair"), 0.0)
        return jnp.where(upper_rows, get(1), get(-1))

    def whole_tile(m, r, x, f):
        if (m, r) == (0, 0):
            return conduct[f][x]
        if (m, r, 0) not in halos:
            return blank
        kind, first, _ = parts_of[m, r, 0]
        if kind == "whole":
            return halos[m, r, 0][x - first, f]
        j, h = divmod(3 * (x - first) + f, 2)
        folded = halos[m, r, 0][j]
        turned = pltpu.roll(folded, ty // 2, 0)
        return jnp.where(second, *((folded, turned) if h else (turned, folded)))

    def pack_tile(m, r, p):
        sides = []
        for c in (1, -1):
            if (m, r, c) not in halos:
                sides.append(blank)
                continue
            got = halos[m, r, c][p]
            kind = parts_of[m, r, c][0]
            if kind == "half strips":
                got = jnp.concatenate([got, got], 0)
            elif kind == "folded strips":
                got = jnp.concatenate([got, pltpu.roll(got, tz // 2, 1)], 0)
            sides.append(got)
        return jnp.where(from_next, *sides)

    merged = {}

    def side_tile(m, beyond, x, f):
        p, n = divmod(x * 3 + f, per)
        if (m, beyond, p) not in merged:
            get = functools.partial(lambda r: pack_tile(m, r, p))
            merged[m, beyond, p] = rows_beyond(get) if beyond else get(0)
        tile2 = merged[m, beyond, p]
        return pltpu.roll(tile2, tz - n * SLOT - SLOT // 2, 1)

    def ring_plane(p, f):
        m, x = divmod(p, tx)
        near = [whole_tile(m, 0, x, f), side_tile(m, False, x, f)]
        far = [rows_beyond(lambda r: whole_tile(m, r, x, f)), side_tile(m, True, x, f)]
        return jnp.concatenate(
            [jnp.concatenate(near, 1), jnp.concatenate(far, 1)], 0
        )

    cond = [
        Slab(lo, jnp.stack([ring_plane(p, f) for p in range(lo, hi)])) for f in range(3)
    ]
    full = 2.0 * (cond[0].data + cond[1].data + cond[2].data)
    inv_total = Slab(lo, jnp.where(full > 0.0, invert(full), 0.0))
    weighted = Slab(lo, sources * inv_total.data)
    third = Slab(lo, inv_total.data * (1.0 / 3.0))
    half_inv = [
        Slab(lo, jnp.where(c.data > 0.0, 0.5 * invert(c.data), 0.0)) for c in cond
    ]

    def own(data, at=0):
        return data[at : at + tx, :ty, :tz]

    def own_of(slab):
        return own(slab.data, -slab.lo)

    def precondition(r, lo, hi):
        shared = (r[0] + r[1] + r[2]) * third.get(lo, hi)
        return [Slab(lo, r[d] * half_inv[d].get(lo, hi) + shared) for d in range(3)]

    hi -= 1
    load = []
    for d in range(3):
        lift = weighted.data + GRAVITY[d] if GRAVITY[d] else weighted.data
        drop = weighted.data - GRAVITY[d] if GRAVITY[d] else weighted.data
        after = following_of(d, Slab(-HALO, cond[d].data * lift), lo, hi)
        load.append(cond[d].get(lo, hi) * drop[: hi - lo] + after)
    vector = precondition(load, lo, hi)
    load = [own(r, -lo) for r in load]
    both = [
        Slab(lo + 1, cond[d].get(lo + 1, hi - 1) + following_of(d, cond[d], lo + 1, hi - 1))
        for d in range(3)
    ]
    basis, images, priors, means = [], [], [], []
    for k in range(ITERS):
        lo += 1
        previous = [previous_of(d, vector[d], lo, hi) for d in range(3)]
        total = sum(
            cond[d].get(lo, hi) * (vector[d].get(lo, hi) + previous[d]) for d in range(3)
        )
        mean = Slab(lo, total * inv_total.get(lo, hi))
        basis.append([own_of(v) for v in vector])
        priors.append([own(p, -lo) for p in previous])
        means.append(mean)
        if k + 1 == ITERS:
            break
        hi -= 1
        image = []
        for d in range(3):
            spread = Slab(lo, cond[d].get(lo, hi + 1) * mean.data)
            image.append(
                both[d].get(lo, hi) * vector[d].get(lo, hi)
                - (spread.get(lo, hi) + following_of(d, spread, lo, hi))
            )
        images.append([own(g, -lo) for g in image])
        fresh = precondition(image, lo, hi)
        vector = [
            Slab(lo, fresh[d].data - SHIFT * vector[d].get(lo, hi)) for d in range(3)
        ]
    center = own_of(means[-1])

    def dot(a, b):
        both = a[0] * b[0] + a[1] * b[1] + a[2] * b[2]
        return sum(both[x] for x in range(tx))

    def place_in(dims):
        slot = 0
        for d in dims:
            slot = slot * counts[d] + here[d]
        return slot

    def send_sum(p, step):
        slot = place_in(phases[p])
        return pltpu.make_async_remote_copy(
            src_ref=sums[p].at[slot],
            dst_ref=sums[p].at[slot],
            send_sem=sum_send.at[p],
            recv_sem=sum_recv.at[p],
            device_id=peer_of(step),
            device_id_type=MESH,
        )

    def all_sums(p, sem):
        others_of = sums[p].at[pl.ds(0, sums[p].shape[0] - 1)]
        return pltpu.make_async_copy(others_of, others_of, sem.at[p])

    at_start = [here[d] * tile[d] + place[d] == 0 for d in range(3)]

    def flux_parts(d, m, m_next, m_back, v, v_back):
        after = conduct[d] * (m - v) + beyond[d] * (v - m_next)
        prior = prior_c[d] * (m_back - v_back) + conduct[d] * (v_back - m)
        return 0.5 * after, jnp.where(at_start[d], 0.0, 0.5 * prior)

    def neighbours(slab):
        after = [own(following_of(d, slab, 0, tx)) for d in range(3)]
        prior = [own(previous_of(d, slab, 0, tx)) for d in range(3)]
        return after, prior

    beyond = [own(following_of(d, cond[d], 0, tx)) for d in range(3)]
    prior_c = [own(previous_of(d, cond[d], 0, tx)) for d in range(3)]

    def prepare():
        state_kept = launch_state(0, state)
        ahead = launch_all(lambda d: ("mean", d), lambda d: [center])
        behind = launch_all(lambda d: ("back", d), lambda d: [center])
        squares = [None] * 3
        cube = cube_moments(state, ratio)
        for d in (1, 0, 2):
            faces = side_faces(0, state, state_kept, d)
            squares[d] = [square_moments(face, ratio) for face in faces]
        moments = cube, squares
        each_halo(-1, lambda message: halo_copy(message).wait_send())
        parts = [[None] * (ITERS + 1) for _ in range(3)]
        w_next, w_back = neighbours(weighted)
        w = own_of(weighted)
        for d in range(3):
            g = GRAVITY[d]
            after = conduct[d] * (w - g) - beyond[d] * (w_next[d] + g)
            prior = prior_c[d] * (w_back[d] - g) - conduct[d] * (w + g)
            parts[d][ITERS] = 0.5 * after, jnp.where(at_start[d], 0.0, 0.5 * prior)
        for k in range(ITERS):
            if k + 1 < ITERS:
                m_next, m_back = neighbours(means[k])
            else:
                m_next = [got[0] for got in land_all(lambda d: ("mean", d), ahead)]
                m_back = [got[0] for got in land_all(lambda d: ("back", d), behind)]
            m = own_of(means[k])
            for d in range(3):
                parts[d][k] = flux_parts(
                    d, m, m_next[d], m_back[d], basis[k][d], priors[k][d]
                )
        return parts, moments

    def side_faces(s, st, kept, d):
        after = land(("down", s, d), kept["down", d])
        prior = land(("up", s, d), kept["up", d])
        return trace(st, d, 1.0), after, prior, trace(st, d, -1.0)

    source = own(sources, HALO)

    rows = [dot(basis[(n + 1) // 2], images[n // 2]) for n in range(2 * ITERS - 2)]
    gaps = [part - center for part in basis[-1] + priors[-1]]
    squares = [conduct[d] * (gaps[d] * gaps[d] + gaps[3 + d] * gaps[3 + d]) for d in range(3)]
    rows.append(sum(squares[0][x] + squares[1][x] + squares[2][x] for x in range(tx)))
    rows.insert(0, dot(basis[0], load))
    acc = jnp.zeros((ty, tz), jnp.float32)
    for r, row in enumerate(rows):
        acc = jnp.where(lane2 == r, jnp.sum(row, axis=1, keepdims=True), acc)
    acc = jnp.sum(acc, axis=0, keepdims=True)
    early = None
    for p, dims in enumerate(phases):
        sums[p][place_in(dims)] = acc
        for step in sorted(peers(dims, counts), key=farness):
            send_sum(p, step).start()
        if early is None:
            early = prepare()
        all_sums(p, sum_recv).wait()
        parts = [sums[p][j] for j in range(sums[p].shape[0])]
        while len(parts) > 1:
            parts = [sum(parts[j : j + 2]) for j in range(0, len(parts), 2)]
        acc = parts[0]
    early = early or prepare()
    parts, moments = early
    acc = jnp.broadcast_to(acc, (ty, tz))
    known = [
        jnp.broadcast_to(
            jnp.sum(jnp.where(lane2 == r, acc, 0.0), axis=1, keepdims=True), (ty, tz)
        )
        for r in range(2 * ITERS)
    ]
    right = [known[0]]
    for i in range(1, ITERS):
        right.append(known[i] - SHIFT * right[-1])
    gram = {(i, j): known[1 + i + j] for i in range(ITERS) for j in range(i, ITERS)}

    factor, pivot = {}, {}
    for i in range(ITERS):
        pivot[i] = invert(gram[i, i])
        for j in range(i + 1, ITERS):
            factor[j, i] = gram[i, j] * pivot[i]
        for j in range(i + 1, ITERS):
            for m in range(j, ITERS):
                gram[j, m] = gram[j, m] - factor[j, i] * gram[i, m]
            right[j] = right[j] - factor[j, i] * right[i]
    coef = [None] * ITERS
    for i in reversed(range(ITERS)):
        value = right[i] * pivot[i]
        for j in range(i + 1, ITERS):
            value = value - factor[j, i] * coef[j]
        coef[i] = value
    coef = [c[None] for c in coef]

    def combine(parts):
        out = coef[0] * parts[0]
        for j in range(1, ITERS):
            out = out + coef[j] * parts[j]
        return out

    fluxes, before = [None] * 3, [None] * 3
    for d in range(3):
        traces_o[d] = combine([p[d] for p in basis])
        fluxes[d] = combine([p[0] for p in parts[d][:ITERS]]) + parts[d][ITERS][0]
        before[d] = combine([p[1] for p in parts[d][:ITERS]]) + parts[d][ITERS][1]
        flux_o[d] = fluxes[d]
    after_pos = [fluxes[d] > 0.0 for d in range(3)]
    before_pos = [before[d] > 0.0 for d in range(3)]
    mid_speed = [0.5 * (before[d] + fluxes[d]) for d in range(3)]
    dif_speed = [0.5 * (fluxes[d] - before[d]) for d in range(3)]

    def pick(flag, a, b):
        return [jnp.where(flag, p, q) for p, q in zip(a, b)]

    def chosen_faces(s, st, kept):
        def across(d):
            upper, after, prior, lower = side_faces(s, st, kept, d)
            return (
                square_moments(pick(after_pos[d], upper, after), ratio),
                square_moments(pick(before_pos[d], prior, lower), ratio),
            )

        def along():
            upper, lower = trace(st, 0, 1.0), trace(st, 0, -1.0)
            last = tx - 1
            o = i = None
            if tx > 1:
                outs = [jnp.where(after_pos[0][:last], u[:last], v[1:]) for u, v in zip(upper, lower)]
                ins = [jnp.where(before_pos[0][1:], u[:last], v[1:]) for u, v in zip(upper, lower)]
                o = square_moments(outs, ratio[:last])
                i = square_moments(ins, ratio[1:])
            after = land_planes(("down", s, 0))
            prior = land_planes(("up", s, 0))
            outs = [jnp.where(after_pos[0][last:], u[last:], a) for u, a in zip(upper, after)]
            ins = [jnp.where(before_pos[0][:1], p, v[:1]) for p, v in zip(prior, lower)]
            o_end = square_moments(outs, ratio[last:])
            i_end = square_moments(ins, ratio[:1])
            if tx == 1:
                return o_end, i_end
            return (
                [jnp.concatenate(pair, 0) for pair in zip(o, o_end)],
                [jnp.concatenate(pair, 0) for pair in zip(i_end, i)],
            )

        return lambda d: along() if d == 0 else across(d)

    def rate(s, st, kept=None, moments=None):
        if moments is None:
            cube = cube_moments(st, ratio)
            find = chosen_faces(s, st, kept)
        else:
            cube, squares = moments

            def find(d):
                upper, after, prior, lower = squares[d]
                return (
                    pick(after_pos[d], upper, after),
                    pick(before_pos[d], prior, lower),
                )

        m1, mlin, msqr, mmix = cube
        out = [jnp.where(source > 0.0, source, source * frac(st[0], ratio))] + [None] * 9
        for d in range(3):
            out[LIN[d]] = 2.0 * (mid_speed[d] * m1 + dif_speed[d] * mlin[d])
            out[SQR[d]] = 6.0 * (mid_speed[d] * mlin[d] + dif_speed[d] * msqr[d])
        for a, b in MIX:
            m = mmix[a, b]
            out[MIX[a, b]] = 2.0 * (
                mid_speed[a] * mlin[b]
                + dif_speed[a] * m
                + mid_speed[b] * mlin[a]
                + dif_speed[b] * m
            )
        for d in (1, 0, 2):
            e, f = others(d)
            outgoing, incoming = find(d)
            o = [fluxes[d] * m for m in outgoing]
            i = [before[d] * m for m in incoming]
            out[0] = out[0] + (i[0] - o[0])
            out[SQR[d]] = out[SQR[d]] + (i[0] - o[0])
            out[LIN[d]] = out[LIN[d]] - (i[0] + o[0])
            out[LIN[e]] = out[LIN[e]] + (i[1] - o[1])
            out[LIN[f]] = out[LIN[f]] + (i[2] - o[2])
            out[mix(d, e)] = out[mix(d, e)] - (i[1] + o[1])
            out[mix(d, f)] = out[mix(d, f)] - (i[2] + o[2])
            out[SQR[e]] = out[SQR[e]] + (i[3] - o[3])
            out[SQR[f]] = out[SQR[f]] + (i[4] - o[4])
            out[mix(e, f)] = out[mix(e, f)] + (i[5] - o[5])
        return [(STEP * MASS[m]) * out[m] for m in range(10)]

    def drain(*kinds):
        for key, m in NAMES.items():
            if key[0] in kinds or len(key) == 3 and key[1] in kinds:

                @pl.when(sends_to(m))
                def _():
                    copy_of(m).wait_send()

    change = rate(0, state, moments=moments)
    first = [state[m] + change[m] for m in range(10)]
    kept = launch_state(1, first)
    drain("mean", "back", 0)
    change = rate(1, first, kept)
    second = [0.75 * state[m] + 0.25 * (first[m] + change[m]) for m in range(10)]
    kept = launch_state(2, second)
    drain(1)
    for p in range(n_sum):
        all_sums(p, sum_send).wait()
    change = rate(2, second, kept)
    for m in range(10):
        sat_o[m] = (1.0 / 3.0) * state[m] + (2.0 / 3.0) * (second[m] + change[m])

    drain(2)


def hand_on(a, b, c, a_out, b_out, c_out):
    a_out[...] = a[...]
    b_out[...] = b[...]
    c_out[...] = c[...]


def per_device(counts, perm, mean0, slopes, rocks, table, wcell, wrate):
    tile = mean0.shape
    f32 = jnp.float32
    bufs = [
        pltpu.VMEM(buffer_shape(dim, f, tile), f32) for dim, _, f in ORDER
    ]
    phases = sum_phases(counts)
    sums = [pltpu.VMEM((len(peers(p, counts)) + 1, 1, tile[2]), f32) for p in phases]
    messages = halo_messages(counts, tile[0])
    parts = [halo_part(m, tile) for m in messages]
    halos = [pltpu.VMEM(part_shape(p, tile), f32) for p in parts]
    made = sorted({p for p in parts if p[0] != "whole"})
    own_halo = [pltpu.VMEM((tile[0], 3) + tile[1:], f32)]
    own_halo += [pltpu.VMEM(part_shape(p, tile), f32) for p in made]
    wcell, wrate = wcell.reshape(1, -1), wrate.reshape(1, -1)
    operands = (perm, mean0, slopes, rocks, table, wcell, wrate)
    copies = [
        (pltpu.SMEM if a is table else pltpu.VMEM)(a.shape, a.dtype) for a in operands
    ]
    vmem = pl.BlockSpec(memory_space=pltpu.VMEM)
    hbm = pl.BlockSpec(memory_space=pltpu.HBM)
    dma = pltpu.SemaphoreType.DMA
    shapes = tuple(jax.ShapeDtypeStruct((n,) + tile, f32) for n in (3, 3, 10))
    results = pl.pallas_call(
        functools.partial(kernel, counts, messages),
        out_shape=tuple(pltpu.VMEM(s.shape, f32) for s in shapes),
        in_specs=[hbm] * len(operands),
        out_specs=(vmem,) * 3,
        scratch_shapes=bufs
        + bufs
        + sums
        + halos
        + own_halo
        + copies
        + [dma((len(ORDER),))] * 2
        + [dma((max(1, len(phases)),))] * 2
        + [dma((len(messages),))] * 2
        + [dma((len(operands),))],
        compiler_params=pltpu.CompilerParams(collective_id=0, has_side_effects=True),
    )(*operands)
    results = [pltpu.with_memory_space_constraint(r, pltpu.VMEM) for r in results]
    return pl.pallas_call(
        hand_on, out_shape=shapes, in_specs=[vmem] * 3, out_specs=(vmem,) * 3
    )(*results)


def solution(mesh):
    counts = tuple(mesh.shape[a] for a in AXES)
    grid = P(None, "gx", "gy", "gz")
    cells = P("gx", "gy", "gz")
    return jax.shard_map(
        functools.partial(per_device, counts),
        mesh=mesh,
        in_specs=(grid, cells, grid, cells, P(), P(), P()),
        out_specs=(grid, grid, grid),
        check_vma=False,
    )
```
